256 devices in a mesh: sta: 32 (over y, z), tpl: 8 (over x, core).
Axes of the slice: x: 4, y: 4, z: 8, core: 2. Of those that a mesh axis runs over, the one named last changes fastest.
Arguments:
- window: bfloat16 [1536, 1024], P('sta', 'tpl'), may hold values from -6 to 6
- prior: bfloat16 [1536, 599], P('sta'), may hold values from -6 to 6
- waves: bfloat16 [256, 128, 600], P('tpl', 'sta'), may hold values from -6 to 6
- chan_list: int32 [256, 128], P('tpl', 'sta'), may hold values from 0 to 1535, as said below
- chan_count: int32 [256], P('tpl'), may hold values from 21 to 120
- station_row: int32 [512], replicated, may hold values from 0 to 511, as said below
Outputs:
- stacked: float32 [256, 1024], P(('tpl', 'sta'))
The draws below stay inside these ranges and needn't reach their ends.
Inputs may be any that keep to these rules, and one draw needn't show every extreme that they name: station_row is a permutation of 0 to 511; station s's three channels are data rows 3 station_row[s] to 3 station_row[s] + 2, and its station block is station_row[s] // 16. `chan_list`: channel c is component c % 3 of station c // 3. For every group of 32 templates (g * 32 to (g + 1) * 32 - 1) and every aligned run of 4 slots, each station block is named by exactly 4 of those slots, listed or not.
All inputs are finite; a program needn't handle non-finite values.
Results may differ from the reference program's by a relative error of at most 0.0029.
Values may be sent and summed in bfloat16 or wider, within the bound.
A program may use at most 64 MiB of HBM per device.

```python
import jax
import jax.numpy as jnp
from jax import lax

TLEN = 600
SLOTS = 128
STA_DEV = 16
LAGS = 1024
STATIONS = 512
CHANNELS = 1536
TPL_GRP = 32
TEMPLATES = 256
SL_DEV = 4
CAP = 4
N_STA = 32
N_TPL = 8


def station_order(key):
    return jax.random.permutation(jax.random.fold_in(key, 11), STATIONS).astype(jnp.int32)


def draw_station_row(key, part):
    return station_order(key)


def draw_chan_list(key, part):
    order_now = station_order(key)
    inverse = jnp.zeros((STATIONS,), jnp.int32).at[order_now].set(jnp.arange(STATIONS, dtype=jnp.int32))
    device_keys = jax.random.split(jax.random.fold_in(key, 23), N_TPL * N_STA)
    shuffles = jax.vmap(lambda one_key: jax.random.permutation(one_key, TPL_GRP * SL_DEV))(device_keys)
    owners = (shuffles // CAP).astype(jnp.int32).reshape(N_TPL, N_STA, TPL_GRP, SL_DEV)
    offset = jax.random.randint(jax.random.fold_in(key, 29), owners.shape, 0, STA_DEV).astype(jnp.int32)
    component = jax.random.randint(jax.random.fold_in(key, 31), owners.shape, 0, 3).astype(jnp.int32)
    station = inverse[owners * STA_DEV + offset]
    channel = 3 * station + component
    return jnp.transpose(channel, (0, 2, 1, 3)).reshape(TEMPLATES, SLOTS).astype(jnp.int32)


def draw_chan_count(key, part):
    lowest = SLOTS // 6
    highest = SLOTS * 15 // 16
    counts = jax.random.randint(jax.random.fold_in(key, 41), (TEMPLATES,), lowest, highest + 1).astype(jnp.int32)
    where_max = jax.random.randint(jax.random.fold_in(key, 43), (), 0, TEMPLATES)
    where_min = (where_max + 1 + jax.random.randint(jax.random.fold_in(key, 47), (), 0, TEMPLATES - 1)) % TEMPLATES
    counts = counts.at[where_max].set(highest)
    counts = counts.at[where_min].set(lowest)
    return counts.astype(jnp.int32)


def block_scale(own_key, extent, pieces, smallest, high):
    factor_of = 1.0
    for dim, blocks in pieces:
        draws = jax.random.uniform(jax.random.fold_in(jax.random.fold_in(own_key, 6), dim), (blocks,), jnp.float32, smallest / len(pieces), high / len(pieces))
        factor_of = factor_of * jnp.repeat(jnp.exp(draws), extent[dim] // blocks).reshape((-1,) + (1,) * (len(extent) - 1 - dim))
    return factor_of


def gaussian(stream_key, extent, scale, limit, cuts=(), held_as=jnp.bfloat16):
    entries = jax.random.normal(stream_key, extent, jnp.float32) * scale
    if len(cuts) > 0:
        entries = block_scale(stream_key, extent, cuts, -0.22, 0.18) * entries
    return jnp.clip(entries, min=-limit, max=limit).astype(held_as)


def setup_inputs(seed: int = 0) -> dict:
    splits = jax.random.split(jax.random.key(seed), 7)
    return {
        "window": gaussian(splits[0], (CHANNELS, LAGS), 1.0, 6.0, ((0, 32), (1, 8))),
        "prior": gaussian(splits[1], (CHANNELS, TLEN - 1), 1.0, 6.0, ((0, 32),)),
        "waves": gaussian(splits[2], (TEMPLATES, SLOTS, TLEN), 1.0, 6.0, ((0, 8), (1, 32))),
        "chan_list": draw_chan_list(jax.random.fold_in(splits[6], 71), 0),
        "chan_count": draw_chan_count(jax.random.fold_in(splits[6], 71), 0),
        "station_row": draw_station_row(jax.random.fold_in(splits[6], 71), 0),
    }


epsilon = 1e-06

def correlate(data_rows, wave_rows):
    result = lax.conv_general_dilated(data_rows[None], wave_rows[:, None, :], (1,), 'VALID', dimension_numbers=('NCH', 'OIH', 'NCH'), feature_group_count=data_rows.shape[0], preferred_element_type=jnp.float32)
    return result[0]

def inverse_energy(rows, lag_count, length):
    squares = rows.astype(jnp.float32) ** 2
    prefix = jnp.concatenate([jnp.zeros((rows.shape[0], 1), jnp.float32), jnp.cumsum(squares, axis=1)], axis=1)
    energy = prefix[:, length:length + lag_count] - prefix[:, :lag_count]
    return 1.0 / jnp.sqrt(energy + epsilon)

def unit_waves(waves, listed):
    raw_wave = waves.astype(jnp.float32)
    wave_norms = jnp.sqrt(lax.optimization_barrier(jnp.sum(raw_wave * raw_wave, axis=-1, keepdims=True)) + epsilon)
    return (raw_wave / wave_norms * listed[..., None]).astype(jnp.bfloat16)

def reference(window, prior, waves, chan_list, chan_count, station_row):
    extended = jnp.concatenate([prior, window], axis=1)
    scales = inverse_energy(extended, LAGS, TLEN)
    listed = (jnp.arange(SLOTS, dtype=jnp.int32)[None, :] < chan_count[:, None]).astype(jnp.float32)
    normed = unit_waves(waves, listed)
    rows_of = (3 * station_row[chan_list // 3] + chan_list % 3).astype(jnp.int32)

    def one_template(inputs):
        rows_here, waves_here = inputs
        traces = correlate(extended[rows_here], waves_here) * scales[rows_here]
        return lax.optimization_barrier(jnp.sum(traces, axis=0))
    return lax.map(one_template, (rows_of, normed))
```

```python
import functools

import jax
import jax.numpy as jnp
from jax import lax
from jax.experimental import pallas as pl
from jax.experimental.pallas import tpu as pltpu
from jax.sharding import PartitionSpec as P

EPSILON = 1e-06
MESH = pl.DeviceIdType.MESH
F32 = jnp.float32
BF16 = jnp.bfloat16
I32 = jnp.int32
NT = (((1,), (1,)), ((), ()))
NN = (((1,), (0,)), ((), ()))

LANES = 128
SUB = 32
QUARTERS = LANES // SUB


def iota(shape, dim):
    return lax.broadcasted_iota(I32, shape, dim)


def dot(a, b, dims):
    return lax.dot_general(a, b, dims, preferred_element_type=F32)


def shift_left(v, n):
    width = v.shape[1]
    return v if n == 0 else pltpu.roll(v, width - n, 1)


def kernel(
    cfg,
    window_ref,
    prior_ref,
    waves_ref,
    chan_ref,
    count_ref,
    table_ref,
    out_ref,
    win,
    flat,
    sbuf,
    rbuf,
    mrow,
    mbuf,
    msm,
    xs,
    xall,
    sc,
    ohl,
    obuf,
    rres,
    win_send,
    win_recv,
    wave_send,
    wave_recv,
    meta_send,
    meta_recv,
    res_send,
    res_recv,
    sm_sem,
):
    n_sta, n_tpl, group, slots, length, rows, lags = cfg
    positions = group * slots
    prior_len = length - 1
    cells = lags // LANES
    k_blocks = pl.cdiv(length + SUB - 1, LANES)
    k_width = k_blocks * LANES
    x_blocks = pl.cdiv(prior_len + lags, LANES)
    pitch = 16
    me = lax.axis_index("sta")
    my_t = lax.axis_index("tpl")

    barrier = pltpu.get_barrier_semaphore()

    def greet_sta(o, _):
        pl.semaphore_signal(
            barrier, inc=1, device_id={"sta": lax.rem(me + o, n_sta)}, device_id_type=MESH
        )
        return 0

    def greet_tpl(o, _):
        pl.semaphore_signal(
            barrier, inc=1, device_id={"tpl": lax.rem(my_t + o, n_tpl)}, device_id_type=MESH
        )
        return 0

    lax.fori_loop(1, n_tpl, greet_tpl, 0)
    lax.fori_loop(1, n_sta, greet_sta, 0)

    square = (positions, positions)
    lane = iota(square, 1)
    sub = iota(square, 0)
    lane1 = iota((1, positions), 1)
    template = lane1 % group

    def to_rows(row):
        return jnp.broadcast_to(row, square).T

    chan = jnp.concatenate([chan_ref[j : j + 1, :] for j in range(slots)], axis=1)
    counts = jnp.concatenate([count_ref[...]] * slots, axis=1)
    station = (chan * 43691) >> 17
    station_rows = to_rows(station)
    looked = jnp.zeros(square, I32)
    for h in range(table_ref.shape[1] // LANES):
        entries = jnp.broadcast_to(table_ref[:, pl.ds(LANES * h, LANES)], square)
        looked = jnp.where(station_rows == lane + LANES * h, entries, looked)
    looked = jnp.sum(looked.T, axis=0, keepdims=True)
    block_stations = rows // 3
    owner = looked // block_stations
    local = 3 * (looked % block_stations) + chan - 3 * station
    cap = positions // n_sta
    before = (to_rows(owner) == owner) & (sub < lane)
    rank = jnp.sum(jnp.where(before, 1, 0), axis=0, keepdims=True)
    slot_at = owner * cap + rank
    place = sub == slot_at
    listed = jnp.where(me * slots + lane1 // group < counts, 1.0, 0.0)
    code_rows = to_rows(local * group + template)
    mrow[...] = jnp.sum(jnp.where(to_rows(slot_at) == lane, code_rows, 0), axis=0, keepdims=True)

    for t in range(0, group):
        wave = waves_ref[t].astype(F32)
        wave = jnp.concatenate([wave, jnp.zeros((slots, k_width - length), F32)], axis=1)
        for r in range(k_blocks):
            flat[r, pl.ds(t, slots, stride=group), :] = wave[:, LANES * r : LANES * (r + 1)]
    mover = jnp.where(place, jnp.broadcast_to(listed, (positions, positions)), 0.0).astype(BF16)
    moved = jnp.concatenate(
        [dot(mover, flat[r].astype(BF16), NN) for r in range(k_blocks)], axis=1
    )
    norms = jnp.sqrt(jnp.sum(moved * moved, axis=1, keepdims=True) + EPSILON)
    normed = moved / norms
    for s in range(n_sta):
        sbuf[s] = normed[cap * s : cap * (s + 1)].astype(BF16)

    pl.semaphore_wait(barrier, n_sta + n_tpl - 2)

    def win_copy(slot, peer):
        return pltpu.make_async_remote_copy(
            src_ref=window_ref,
            dst_ref=win.at[slot],
            send_sem=win_send.at[peer],
            recv_sem=win_recv.at[slot],
            device_id={"tpl": peer},
            device_id_type=MESH,
        )

    def wave_copy(slot, peer):
        return pltpu.make_async_remote_copy(
            src_ref=sbuf.at[peer],
            dst_ref=rbuf.at[slot],
            send_sem=wave_send.at[peer],
            recv_sem=wave_recv.at[slot],
            device_id={"sta": peer},
            device_id_type=MESH,
        )

    def meta_copy(slot, peer):
        return pltpu.make_async_remote_copy(
            src_ref=mrow,
            dst_ref=mbuf.at[slot],
            send_sem=meta_send.at[peer],
            recv_sem=meta_recv.at[slot],
            device_id={"sta": peer},
            device_id_type=MESH,
        )

    def res_copy(slot, peer):
        return pltpu.make_async_remote_copy(
            src_ref=obuf.at[peer],
            dst_ref=rres.at[slot],
            send_sem=res_send.at[peer],
            recv_sem=res_recv.at[slot],
            device_id={"sta": peer},
            device_id_type=MESH,
        )

    def over(count, first, body):
        def step(o, _):
            body(lax.rem(first + o, count))
            return 0

        lax.fori_loop(1, count, step, 0)

    over(n_tpl, my_t, lambda peer: win_copy(my_t, peer).start())

    def send_waves(peer):
        meta_copy(me, peer).start()
        wave_copy(me, peer).start()

    over(n_sta, me, send_waves)
    win[my_t] = window_ref[...]
    rbuf[me] = sbuf[me]
    mbuf[me] = mrow[...]

    over(n_tpl, my_t, lambda peer: win_copy(peer, peer).wait_recv())

    lane_p = iota((8, LANES), 1)
    prior_tiles = prior_len // LANES
    prior_rest = prior_len % LANES

    for g in range(rows // 8):
        r8 = pl.ds(8 * g, 8)
        old = prior_ref[r8, :].astype(F32)
        new = jnp.concatenate(
            [win[p, r8, :].astype(F32) for p in range(n_tpl)] + [jnp.zeros((8, LANES), F32)], axis=1
        )
        new = pltpu.roll(new, prior_rest, 1)
        tail = jnp.concatenate(
            [old[:, prior_tiles * LANES :], jnp.zeros((8, LANES - prior_rest), F32)], axis=1
        )
        joint = jnp.where(lane_p < prior_rest, tail, new[:, :LANES])
        x = jnp.concatenate([old[:, : prior_tiles * LANES], joint, new[:, LANES:]], axis=1)
        for b in range(QUARTERS):
            moved_x = shift_left(x, SUB * b)
            for m in range(x_blocks):
                xs[b, pl.ds(pitch * 8 * g + m, 8, stride=pitch), :] = moved_x[
                    :, LANES * m : LANES * (m + 1)
                ]
        sums = {1: x * x}
        size = 1
        while 2 * size <= length:
            sums[2 * size] = sums[size] + shift_left(sums[size], size)
            size *= 2
        energy, done = None, 0
        while size:
            if length & size:
                part = shift_left(sums[size], done)
                energy = part if energy is None else energy + part
                done += size
            size //= 2
        scale = 1.0 / jnp.sqrt(energy[:, :lags] + EPSILON)
        for a in range(cells):
            sc[r8, a, :] = scale[:, LANES * a : LANES * (a + 1)]

    def build_row(c, _):
        for r in range(k_blocks):
            for b in range(0, QUARTERS, 2):
                pair = jnp.concatenate(
                    [xs[b + d, pl.ds(pitch * c + r, cells), :] for d in range(2)], axis=0
                )
                xall[c, pl.ds(cells * b, 2 * cells), pl.ds(LANES * r, LANES)] = pair.astype(BF16)
        return 0

    lax.fori_loop(0, rows, build_row, 0)

    def take(peer):
        meta_copy(peer, peer).wait_recv()
        wave_copy(peer, peer).wait_recv()

    over(n_sta, me, take)
    to_sm = pltpu.make_async_copy(mbuf, msm, sm_sem)
    to_sm.start()
    to_sm.wait()

    quarter = iota((8, LANES), 1) // SUB

    def pick(parts):
        value = parts[0]
        for i in range(1, QUARTERS):
            value = jnp.where(quarter == i, parts[i], value)
        return value

    def correlate(s, _):
        wave = rbuf[s].astype(F32)
        codes = [msm[s, 0, cap * me + i] for i in range(cap)]
        local_rows = [code >> (group.bit_length() - 1) for code in codes]
        shifted = jnp.concatenate(
            [
                pltpu.roll(
                    jnp.broadcast_to(wave[i : i + 1], (SUB, k_width)), 0, 1, stride=1, stride_axis=0
                )
                for i in range(cap)
            ],
            axis=0,
        ).astype(BF16)
        data = jnp.concatenate([xall[c] for c in local_rows], axis=0)
        found = dot(data, shifted, NT)
        block = lambda i, b: found[SUB * i + cells * b : SUB * i + cells * (b + 1)]
        turned = []
        for d in range(QUARTERS):
            v = pick([block(i, (i + d) % QUARTERS) for i in range(cap)])
            turned.append(v if d == 0 else pltpu.roll(v, SUB * d, 1))
        out = []
        for i in range(cap):
            v = pick([turned[(b - i) % QUARTERS] for b in range(QUARTERS)])
            out.append(v * sc[local_rows[i]])
        traces = jnp.concatenate(out, axis=0)
        hi = traces.astype(BF16)
        lo = (traces - hi.astype(F32)).astype(BF16)
        here = pl.ds(pl.multiple_of(cells * cap * s, cells * cap), cells * cap)
        ohl[here, pl.ds(0, LANES)] = hi
        ohl[here, pl.ds(LANES, LANES)] = lo
        return 0

    lax.fori_loop(0, n_sta, correlate, 0)

    codes = mbuf[...].reshape(n_sta, LANES)
    mine = pltpu.roll(codes, lax.rem(positions - cap * me, positions), 1)
    tmpl = mine & (group - 1)
    lane_s = iota((n_sta, LANES), 1)
    sub_s = iota((n_sta, LANES), 0)
    by_lane = jnp.zeros((n_sta, LANES), I32)
    for j in range(cap):
        by_lane = jnp.where(
            (lane_s // cells) % cap == j, jnp.broadcast_to(tmpl[:, j : j + 1], (n_sta, LANES)), by_lane
        )
    per_tile = LANES // (cap * cells)
    by_lane = by_lane.astype(F32)
    out_rows = group * cells
    row_t = (iota((out_rows, LANES), 0) // cells).astype(F32)
    same_a = iota((out_rows, LANES), 0) % cells == iota((out_rows, LANES), 1) % cells
    tiles = []
    for m in range(positions * cells // LANES):
        names = jnp.sum(
            jnp.where(sub_s == per_tile * m + lane_s // (cap * cells), by_lane, 0.0),
            axis=0,
            keepdims=True,
        )
        tiles.append(jnp.where((row_t == names) & same_a, 1.0, 0.0).astype(BF16))
    chooser = jnp.concatenate(tiles, axis=1)
    both = dot(chooser, ohl[...], NN)
    stacked = both[:, :LANES] + both[:, LANES:]
    for t in range(group):
        obuf[t] = stacked[cells * t : cells * (t + 1)]

    over(n_sta, me, lambda peer: res_copy(me, peer).start())
    rres[me] = obuf[me]
    over(n_sta, me, lambda peer: res_copy(peer, peer).wait_recv())
    total = jnp.sum(rres[...], axis=0)
    for a in range(cells):
        out_ref[0:1, pl.ds(LANES * a, LANES)] = total[a : a + 1]

    over(n_tpl, my_t, lambda peer: win_copy(my_t, peer).wait_send())

    def drain(peer):
        meta_copy(me, peer).wait_send()
        wave_copy(me, peer).wait_send()
        res_copy(me, peer).wait_send()

    over(n_sta, me, drain)


def solution(mesh):
    n_sta, n_tpl = mesh.shape["sta"], mesh.shape["tpl"]

    def per_device(window, prior, waves, chan_list, chan_count, station_row):
        group, slots, length = waves.shape
        rows = window.shape[0]
        lags = window.shape[1] * n_tpl
        positions = group * slots
        cap = positions // n_sta
        cells = lags // LANES
        k_width = pl.cdiv(length + SUB - 1, LANES) * LANES
        cfg = (n_sta, n_tpl, group, slots, length, rows, lags)
        vmem = pl.BlockSpec(memory_space=pltpu.VMEM)
        dma = pltpu.SemaphoreType.DMA
        return pl.pallas_call(
            functools.partial(kernel, cfg),
            out_shape=jax.ShapeDtypeStruct((1, lags), F32),
            in_specs=[vmem] * 6,
            out_specs=vmem,
            scratch_shapes=[
                pltpu.VMEM((n_tpl, rows, window.shape[1]), BF16),
                pltpu.VMEM((k_width // LANES, positions, LANES), F32),
                pltpu.VMEM((n_sta, cap, k_width), BF16),
                pltpu.VMEM((n_sta, cap, k_width), BF16),
                pltpu.VMEM((1, positions), I32),
                pltpu.VMEM((n_sta, 1, positions), I32),
                pltpu.SMEM((n_sta, 1, positions), I32),
                pltpu.VMEM((QUARTERS, rows * 16, LANES), F32),
                pltpu.VMEM((rows, SUB, k_width), BF16),
                pltpu.VMEM((rows, cells, LANES), F32),
                pltpu.VMEM((positions * cells, 2 * LANES), BF16),
                pltpu.VMEM((group, cells, LANES), F32),
                pltpu.VMEM((n_sta, cells, LANES), F32),
                dma((n_tpl,)),
                dma((n_tpl,)),
                dma((n_sta,)),
                dma((n_sta,)),
                dma((n_sta,)),
                dma((n_sta,)),
                dma((n_sta,)),
                dma((n_sta,)),
                dma(()),
            ],
            compiler_params=pltpu.CompilerParams(collective_id=0, has_side_effects=True),
        )(
            window,
            prior,
            waves,
            chan_list.T,
            chan_count.reshape(1, group),
            station_row.reshape(1, -1),
        )

    return jax.shard_map(
        per_device,
        mesh=mesh,
        in_specs=(
            P("sta", "tpl"),
            P("sta", None),
            P("tpl", "sta", None),
            P("tpl", "sta"),
            P("tpl"),
            P(),
        ),
        out_specs=P(("tpl", "sta"), None),
        check_vma=False,
    )
```

```python
import functools

import jax
import jax.numpy as jnp
from jax import lax
from jax.experimental import pallas as pl
from jax.experimental.pallas import tpu as pltpu
from jax.sharding import PartitionSpec as P

EPSILON = 1e-06
MESH = pl.DeviceIdType.MESH
F32 = jnp.float32
BF16 = jnp.bfloat16
I32 = jnp.int32
NT = (((1,), (1,)), ((), ()))
NN = (((1,), (0,)), ((), ()))

LANES = 128
SUB = 32
BATCH = 8
QUARTERS = LANES // SUB


def iota(shape, dim):
    return lax.broadcasted_iota(I32, shape, dim)


def dot(a, b, dims):
    return lax.dot_general(a, b, dims, preferred_element_type=F32)


def shift_left(v, n):
    width = v.shape[1]
    return v if n == 0 else pltpu.roll(v, width - n, 1)


def kernel(
    cfg,
    window_hbm,
    prior_hbm,
    waves_hbm,
    chan_hbm,
    count_hbm,
    table_hbm,
    out_ref,
    window_ref,
    prior_ref,
    waves_ref,
    chan_ref,
    count_ref,
    table_ref,
    win,
    flat,
    sbuf,
    rbuf,
    mrow,
    mbuf,
    msm,
    xs,
    xall,
    sc,
    ohl,
    obuf,
    rres,
    win_send,
    win_recv,
    wave_send,
    wave_recv,
    meta_send,
    meta_recv,
    res_send,
    res_recv,
    sm_sem,
    in_sem,
):
    n_sta, n_tpl, group, slots, length, rows, lags, z_size = cfg
    positions = group * slots
    prior_len = length - 1
    cells = lags // LANES
    k_blocks = pl.cdiv(length + SUB - 1, LANES)
    k_width = k_blocks * LANES
    x_blocks = pl.cdiv(prior_len + lags, LANES)
    pitch = x_blocks
    me = lax.axis_index("sta")
    my_t = lax.axis_index("tpl")

    my_y, my_z = me // z_size, me % z_size
    y_size = n_sta // z_size

    def peer_of(k):
        i, j = k // y_size, k % y_size
        dz = z_size // 2 + jnp.where(i % 2 == 1, -((i + 1) // 2), i // 2)
        dy = y_size // 2 + jnp.where(j % 2 == 1, -((j + 1) // 2), j // 2)
        return ((my_y + dy) % y_size) * z_size + (my_z + dz) % z_size

    barrier = pltpu.get_barrier_semaphore()

    def greet_sta(k, _):
        pl.semaphore_signal(barrier, inc=1, device_id={"sta": peer_of(k)}, device_id_type=MESH)
        return 0

    def greet_tpl(o, _):
        pl.semaphore_signal(
            barrier, inc=1, device_id={"tpl": lax.rem(my_t + o, n_tpl)}, device_id_type=MESH
        )
        return 0

    inputs = [
        pltpu.make_async_copy(src, dst, in_sem.at[n])
        for n, (src, dst) in enumerate(
            [
                (chan_hbm, chan_ref),
                (count_hbm, count_ref),
                (table_hbm, table_ref),
                (waves_hbm, waves_ref),
                (window_hbm, window_ref),
                (prior_hbm, prior_ref),
            ]
        )
    ]
    for copy in inputs:
        copy.start()
    lax.fori_loop(0, n_sta - 1, greet_sta, 0)
    lax.fori_loop(1, n_tpl, greet_tpl, 0)
    for copy in inputs:
        copy.wait()

    square = (positions, positions)
    lane = iota(square, 1)
    sub = iota(square, 0)
    lane1 = iota((1, positions), 1)
    template = lane1 % group

    def to_rows(row):
        return jnp.broadcast_to(row, square).T

    chan = jnp.concatenate([chan_ref[j : j + 1, :] for j in range(slots)], axis=1)
    counts = jnp.concatenate([count_ref[...]] * slots, axis=1)
    station = (chan * 43691) >> 17
    station_rows = to_rows(station)
    looked = jnp.zeros(square, I32)
    for h in range(table_ref.shape[1] // LANES):
        entries = jnp.broadcast_to(table_ref[:, pl.ds(LANES * h, LANES)], square)
        looked = jnp.where(station_rows == lane + LANES * h, entries, looked)
    looked = jnp.sum(looked.T, axis=0, keepdims=True)
    block_stations = rows // 3
    owner = looked // block_stations
    local = 3 * (looked % block_stations) + chan - 3 * station
    cap = positions // n_sta
    before = (to_rows(owner) == owner) & (sub < lane)
    rank = jnp.sum(jnp.where(before, 1, 0), axis=0, keepdims=True)
    slot_at = owner * cap + rank
    place = sub == slot_at
    listed = jnp.where(me * slots + lane1 // group < counts, 1.0, 0.0)
    code_rows = to_rows(local * group + template)
    mrow[...] = jnp.sum(jnp.where(to_rows(slot_at) == lane, code_rows, 0), axis=0, keepdims=True)

    for t in range(0, group):
        wave = waves_ref[t].astype(F32)
        wave = jnp.concatenate([wave, jnp.zeros((slots, k_width - length), F32)], axis=1)
        for r in range(k_blocks):
            flat[r, pl.ds(t, slots, stride=group), :] = wave[:, LANES * r : LANES * (r + 1)]
    mover = jnp.where(place, jnp.broadcast_to(listed, (positions, positions)), 0.0).astype(BF16)
    moved = jnp.concatenate(
        [dot(mover, flat[r].astype(BF16), NN) for r in range(k_blocks)], axis=1
    )
    norms = jnp.sqrt(jnp.sum(moved * moved, axis=1, keepdims=True) + EPSILON)
    normed = moved / norms
    for s in range(n_sta):
        sbuf[s] = normed[cap * s : cap * (s + 1)].astype(BF16)

    pl.semaphore_wait(barrier, n_sta + n_tpl - 2)

    def remote(src, dst, send, recv, device):
        return pltpu.make_async_remote_copy(
            src_ref=src,
            dst_ref=dst,
            send_sem=send,
            recv_sem=recv,
            device_id=device,
            device_id_type=MESH,
        )

    def win_copy(slot, peer):
        return remote(window_ref, win.at[slot], win_send.at[peer], win_recv.at[slot], {"tpl": peer})

    def wave_copy(k, peer):
        return remote(
            sbuf.at[peer], rbuf.at[k], wave_send, wave_recv.at[k // BATCH], {"sta": peer}
        )

    def meta_copy(k, peer):
        return remote(
            mrow, mbuf.at[k], meta_send, meta_recv.at[k // BATCH], {"sta": peer}
        )

    def res_copy(k, peer):
        return remote(obuf.at[peer], rres.at[k], res_send, res_recv, {"sta": peer})

    def over_tpl(body):
        def step(o, _):
            body(lax.rem(my_t + o, n_tpl))
            return 0

        lax.fori_loop(1, n_tpl, step, 0)

    def over_sta(body):
        def step(k, _):
            body(k, peer_of(k))
            return 0

        lax.fori_loop(0, n_sta - 1, step, 0)

    batches = n_sta // BATCH

    def batch_of(g):
        return pl.ds(BATCH * g, BATCH - 1 if g == batches - 1 else BATCH)

    over_sta(lambda k, peer: meta_copy(k, peer).start())
    over_tpl(lambda peer: win_copy(my_t, peer).start())
    over_sta(lambda k, peer: wave_copy(k, peer).start())
    win[my_t] = window_ref[...]
    rbuf[n_sta - 1] = sbuf[me]
    mbuf[n_sta - 1] = mrow[...]

    over_tpl(lambda peer: win_copy(peer, peer).wait_recv())

    lane_p = iota((8, LANES), 1)
    prior_tiles = prior_len // LANES
    prior_rest = prior_len % LANES

    for g in range(rows // 8):
        r8 = pl.ds(8 * g, 8)
        old = prior_ref[r8, :].astype(F32)
        new = jnp.concatenate(
            [win[p, r8, :].astype(F32) for p in range(n_tpl)] + [jnp.zeros((8, LANES), F32)], axis=1
        )
        new = pltpu.roll(new, prior_rest, 1)
        tail = jnp.concatenate(
            [old[:, prior_tiles * LANES :], jnp.zeros((8, LANES - prior_rest), F32)], axis=1
        )
        joint = jnp.where(lane_p < prior_rest, tail, new[:, :LANES])
        x = jnp.concatenate([old[:, : prior_tiles * LANES], joint, new[:, LANES:]], axis=1)
        for b in range(QUARTERS):
            moved_x = shift_left(x, SUB * b)
            for m in range(x_blocks):
                xs[b, pl.ds(pitch * 8 * g + m, 8, stride=pitch), :] = moved_x[
                    :, LANES * m : LANES * (m + 1)
                ]
        sums = {1: x * x}
        size = 1
        while 2 * size <= length:
            sums[2 * size] = sums[size] + shift_left(sums[size], size)
            size *= 2
        energy, done = None, 0
        while size:
            if length & size:
                part = shift_left(sums[size], done)
                energy = part if energy is None else energy + part
                done += size
            size //= 2
        scale = 1.0 / jnp.sqrt(energy[:, :lags] + EPSILON)
        for a in range(cells):
            sc[r8, a, :] = scale[:, LANES * a : LANES * (a + 1)]

    def build_row(c, _):
        for r in range(k_blocks):
            for b in range(0, QUARTERS, 2):
                pair = jnp.concatenate(
                    [xs[b + d, pl.ds(pitch * c + r, cells), :] for d in range(2)], axis=0
                )
                xall[c, pl.ds(cells * b, 2 * cells), pl.ds(LANES * r, LANES)] = pair.astype(BF16)
        return 0

    lax.fori_loop(0, rows, build_row, 0, unroll=4)

    quarter = iota((8, LANES), 1) // SUB

    def pick(parts):
        value = parts[0]
        for i in range(1, QUARTERS):
            value = jnp.where(quarter == i, parts[i], value)
        return value

    def correlate(s):
        wave = rbuf[s].astype(F32)
        codes = [msm[s, 0, cap * me + i] for i in range(cap)]
        local_rows = [code >> (group.bit_length() - 1) for code in codes]
        shifted = jnp.concatenate(
            [
                pltpu.roll(
                    jnp.broadcast_to(wave[i : i + 1], (SUB, k_width)), 0, 1, stride=1, stride_axis=0
                )
                for i in range(cap)
            ],
            axis=0,
        ).astype(BF16)
        data = jnp.concatenate([xall[c] for c in local_rows], axis=0)
        found = dot(data, shifted, NT)
        block = lambda i, b: found[SUB * i + cells * b : SUB * i + cells * (b + 1)]
        turned = []
        for d in range(QUARTERS):
            v = pick([block(i, (i + d) % QUARTERS) for i in range(cap)])
            turned.append(v if d == 0 else pltpu.roll(v, SUB * d, 1))
        out = []
        for i in range(cap):
            v = pick([turned[(b - i) % QUARTERS] for b in range(QUARTERS)])
            out.append(v * sc[local_rows[i]])
        traces = jnp.concatenate(out, axis=0)
        hi = traces.astype(BF16)
        lo = (traces - hi.astype(F32)).astype(BF16)
        here = pl.ds(cells * cap * s, cells * cap)
        ohl[here, pl.ds(0, LANES)] = hi
        ohl[here, pl.ds(LANES, LANES)] = lo

    def to_scalars(g):
        here = pl.ds(BATCH * g, BATCH)
        return pltpu.make_async_copy(mbuf.at[here], msm.at[here], sm_sem.at[g])

    def meta_here(g):
        here = batch_of(g)
        remote(mbuf.at[here], mbuf.at[here], meta_send, meta_recv.at[g], {"sta": me}).wait_recv()
        to_scalars(g).start()

    def waves_here(g):
        here = batch_of(g)
        remote(rbuf.at[here], rbuf.at[here], wave_send, wave_recv.at[g], {"sta": me}).wait_recv()

    meta_here(batches - 1)
    for g in reversed(range(batches)):
        if g:
            meta_here(g - 1)
        waves_here(g)
        to_scalars(g).wait()
        for k in range(BATCH):
            correlate(BATCH * g + k)

    codes = mbuf[...].reshape(n_sta, LANES)
    mine = pltpu.roll(codes, lax.rem(positions - cap * me, positions), 1)
    tmpl = mine & (group - 1)
    lane_s = iota((n_sta, LANES), 1)
    sub_s = iota((n_sta, LANES), 0)
    by_lane = jnp.zeros((n_sta, LANES), I32)
    for j in range(cap):
        by_lane = jnp.where(
            (lane_s // cells) % cap == j, jnp.broadcast_to(tmpl[:, j : j + 1], (n_sta, LANES)), by_lane
        )
    per_tile = LANES // (cap * cells)
    by_lane = by_lane.astype(F32)
    out_rows = group * cells
    row_t = (iota((out_rows, LANES), 0) // cells).astype(F32)
    same_a = iota((out_rows, LANES), 0) % cells == iota((out_rows, LANES), 1) % cells
    tiles = []
    for m in range(positions * cells // LANES):
        names = jnp.sum(
            jnp.where(sub_s == per_tile * m + lane_s // (cap * cells), by_lane, 0.0),
            axis=0,
            keepdims=True,
        )
        tiles.append(jnp.where((row_t == names) & same_a, 1.0, 0.0).astype(BF16))
    chooser = jnp.concatenate(tiles, axis=1)
    both = dot(chooser, ohl[...], NN)
    stacked = both[:, :LANES] + both[:, LANES:]
    for t in range(group):
        obuf[t] = stacked[cells * t : cells * (t + 1)]

    over_sta(lambda k, peer: res_copy(k, peer).start())
    rres[n_sta - 1] = obuf[me]
    others = pl.ds(0, n_sta - 1)
    over_tpl(lambda peer: win_copy(my_t, peer).wait_send())
    remote(mbuf.at[others], mbuf.at[others], meta_send, meta_recv.at[0], {"sta": me}).wait_send()
    remote(sbuf.at[others], sbuf.at[others], wave_send, wave_recv.at[0], {"sta": me}).wait_send()
    results = remote(obuf.at[others], rres.at[others], res_send, res_recv, {"sta": me})
    results.wait_send()
    results.wait_recv()
    total = jnp.sum(rres[...], axis=0)
    for a in range(cells):
        out_ref[0:1, pl.ds(LANES * a, LANES)] = total[a : a + 1]


def solution(mesh):
    n_sta, n_tpl = mesh.shape["sta"], mesh.shape["tpl"]

    def per_device(window, prior, waves, chan_list, chan_count, station_row):
        group, slots, length = waves.shape
        rows = window.shape[0]
        lags = window.shape[1] * n_tpl
        positions = group * slots
        cap = positions // n_sta
        cells = lags // LANES
        k_width = pl.cdiv(length + SUB - 1, LANES) * LANES
        cfg = (n_sta, n_tpl, group, slots, length, rows, lags, 8)
        vmem = pl.BlockSpec(memory_space=pltpu.VMEM)
        dma = pltpu.SemaphoreType.DMA
        return pl.pallas_call(
            functools.partial(kernel, cfg),
            out_shape=jax.ShapeDtypeStruct((1, lags), F32),
            in_specs=[pl.BlockSpec(memory_space=pl.ANY)] * 6,
            out_specs=vmem,
            scratch_shapes=[
                pltpu.VMEM(window.shape, BF16),
                pltpu.VMEM(prior.shape, BF16),
                pltpu.VMEM(waves.shape, BF16),
                pltpu.VMEM((slots, group), I32),
                pltpu.VMEM((1, group), I32),
                pltpu.VMEM((1, station_row.shape[0]), I32),
                pltpu.VMEM((n_tpl, rows, window.shape[1]), BF16),
                pltpu.VMEM((k_width // LANES, positions, LANES), F32),
                pltpu.VMEM((n_sta, cap, k_width), BF16),
                pltpu.VMEM((n_sta, cap, k_width), BF16),
                pltpu.VMEM((1, positions), I32),
                pltpu.VMEM((n_sta, 1, positions), I32),
                pltpu.SMEM((n_sta, 1, positions), I32),
                pltpu.VMEM((QUARTERS, rows * pl.cdiv(length - 1 + lags, LANES), LANES), F32),
                pltpu.VMEM((rows, SUB, k_width), BF16),
                pltpu.VMEM((rows, cells, LANES), F32),
                pltpu.VMEM((positions * cells, 2 * LANES), BF16),
                pltpu.VMEM((group, cells, LANES), F32),
                pltpu.VMEM((n_sta, cells, LANES), F32),
                dma((n_tpl,)),
                dma((n_tpl,)),
                dma(()),
                dma((n_sta // BATCH,)),
                dma(()),
                dma((n_sta // BATCH,)),
                dma(()),
                dma(()),
                dma((n_sta // BATCH,)),
                dma((6,)),
            ],
            compiler_params=pltpu.CompilerParams(collective_id=0, has_side_effects=True),
        )(
            window,
            prior,
            waves,
            chan_list.T,
            chan_count.reshape(1, group),
            station_row.reshape(1, -1),
        )

    return jax.shard_map(
        per_device,
        mesh=mesh,
        in_specs=(
            P("sta", "tpl"),
            P("sta", None),
            P("tpl", "sta", None),
            P("tpl", "sta"),
            P("tpl"),
            P(),
        ),
        out_specs=P(("tpl", "sta"), None),
        check_vma=False,
    )
```

```python
import functools

import jax
import jax.numpy as jnp
from jax import lax
from jax.experimental import pallas as pl
from jax.experimental.pallas import tpu as pltpu
from jax.sharding import PartitionSpec as P

EPSILON = 1e-06
MESH = pl.DeviceIdType.MESH
F32 = jnp.float32
BF16 = jnp.bfloat16
I32 = jnp.int32
NT = (((1,), (1,)), ((), ()))
NN = (((1,), (0,)), ((), ()))

LANES = 128
SUB = 32
BATCH = 8
QUARTERS = LANES // SUB


def iota(shape, dim):
    return lax.broadcasted_iota(I32, shape, dim)


def dot(a, b, dims):
    return lax.dot_general(a, b, dims, preferred_element_type=F32)


def shift_left(v, n):
    width = v.shape[1]
    return v if n == 0 else pltpu.roll(v, width - n, 1)


def kernel(
    cfg,
    window_hbm,
    prior_hbm,
    waves_hbm,
    chan_hbm,
    count_hbm,
    table_hbm,
    out_ref,
    window_ref,
    prior_ref,
    waves_ref,
    chan_ref,
    count_ref,
    table_ref,
    win,
    flat,
    sbuf,
    rbuf,
    mrow,
    mbuf,
    msm,
    xs,
    xall,
    sc,
    ohl,
    obuf,
    rres,
    win_send,
    win_recv,
    wave_send,
    wave_recv,
    meta_send,
    meta_recv,
    res_send,
    res_recv,
    sm_sem,
    in_sem,
):
    n_sta, n_tpl, group, slots, length, rows, lags, z_size = cfg
    positions = group * slots
    prior_len = length - 1
    cells = lags // LANES
    k_blocks = pl.cdiv(length + SUB - 1, LANES)
    k_width = k_blocks * LANES
    x_blocks = pl.cdiv(prior_len + lags, LANES)
    pitch = x_blocks
    me = lax.axis_index("sta")
    my_t = lax.axis_index("tpl")

    y_size = n_sta // z_size
    my_y = lax.div(me, z_size)
    my_z = me - my_y * z_size

    def outward(n):
        return sorted(range(n), key=lambda d: -min(d, n - d))

    at_z = [lax.rem(my_z + d, z_size) for d in outward(z_size)]
    at_y = [lax.rem(my_y + d, y_size) * z_size for d in outward(y_size)]
    peers = [z + y for z in at_z for y in at_y][: n_sta - 1]
    tpl_peers = [lax.rem(my_t + o, n_tpl) for o in range(1, n_tpl)]

    barrier = pltpu.get_barrier_semaphore()

    inputs = [
        pltpu.make_async_copy(src, dst, in_sem.at[n])
        for n, (src, dst) in enumerate(
            [
                (chan_hbm, chan_ref),
                (count_hbm, count_ref),
                (table_hbm, table_ref),
                (waves_hbm, waves_ref),
                (window_hbm, window_ref),
                (prior_hbm, prior_ref),
            ]
        )
    ]
    for copy in inputs:
        copy.start()
    for peer in peers:
        pl.semaphore_signal(barrier, inc=1, device_id={"sta": peer}, device_id_type=MESH)
    for peer in tpl_peers:
        pl.semaphore_signal(barrier, inc=1, device_id={"tpl": peer}, device_id_type=MESH)
    for copy in inputs:
        copy.wait()

    square = (positions, positions)
    lane = iota(square, 1)
    sub = iota(square, 0)
    lane1 = iota((1, positions), 1)
    template = lane1 % group

    def to_rows(row):
        return jnp.broadcast_to(row, square).T

    chan = jnp.concatenate([chan_ref[j : j + 1, :] for j in range(slots)], axis=1)
    counts = jnp.concatenate([count_ref[...]] * slots, axis=1)
    station = (chan * 43691) >> 17
    station_rows = to_rows(station)
    looked = jnp.zeros(square, I32)
    for h in range(table_ref.shape[1] // LANES):
        entries = jnp.broadcast_to(table_ref[:, pl.ds(LANES * h, LANES)], square)
        looked = jnp.where(station_rows == lane + LANES * h, entries, looked)
    looked = jnp.sum(looked.T, axis=0, keepdims=True)
    block_stations = rows // 3
    owner = looked // block_stations
    local = 3 * (looked % block_stations) + chan - 3 * station
    cap = positions // n_sta
    before = (to_rows(owner) == owner) & (sub < lane)
    rank = jnp.sum(jnp.where(before, 1, 0), axis=0, keepdims=True)
    slot_at = owner * cap + rank
    place = sub == slot_at
    listed = jnp.where(me * slots + lane1 // group < counts, 1.0, 0.0)
    code_rows = to_rows(local * group + template)
    mrow[...] = jnp.sum(jnp.where(to_rows(slot_at) == lane, code_rows, 0), axis=0, keepdims=True)

    for t in range(0, group):
        wave = waves_ref[t].astype(F32)
        wave = jnp.concatenate([wave, jnp.zeros((slots, k_width - length), F32)], axis=1)
        for r in range(k_blocks):
            flat[r, pl.ds(t, slots, stride=group), :] = wave[:, LANES * r : LANES * (r + 1)]
    mover = jnp.where(place, jnp.broadcast_to(listed, (positions, positions)), 0.0).astype(BF16)
    moved = jnp.concatenate(
        [dot(mover, flat[r].astype(BF16), NN) for r in range(k_blocks)], axis=1
    )
    norms = jnp.sqrt(jnp.sum(moved * moved, axis=1, keepdims=True) + EPSILON)
    normed = moved / norms
    for s in range(n_sta):
        sbuf[s] = normed[cap * s : cap * (s + 1)].astype(BF16)

    pl.semaphore_wait(barrier, n_sta + n_tpl - 2)

    def remote(src, dst, send, recv, device):
        return pltpu.make_async_remote_copy(
            src_ref=src,
            dst_ref=dst,
            send_sem=send,
            recv_sem=recv,
            device_id=device,
            device_id_type=MESH,
        )

    def win_copy(slot, peer):
        return remote(window_ref, win.at[slot], win_send.at[peer], win_recv.at[slot], {"tpl": peer})

    def wave_copy(k, peer):
        return remote(
            sbuf.at[peer], rbuf.at[k], wave_send, wave_recv.at[k // BATCH], {"sta": peer}
        )

    def meta_copy(k, peer):
        return remote(
            mrow, mbuf.at[k], meta_send, meta_recv.at[k // BATCH], {"sta": peer}
        )

    def res_copy(k, peer):
        return remote(obuf.at[peer], rres.at[k], res_send, res_recv, {"sta": peer})

    def over_tpl(body):
        for peer in tpl_peers:
            body(peer)

    def over_sta(body):
        for k, peer in enumerate(peers):
            body(k, peer)

    batches = n_sta // BATCH

    def batch_of(g):
        return pl.ds(BATCH * g, BATCH - 1 if g == batches - 1 else BATCH)

    over_tpl(lambda peer: win_copy(my_t, peer).start())
    over_sta(lambda k, peer: meta_copy(k, peer).start())
    over_sta(lambda k, peer: wave_copy(k, peer).start())
    win[my_t] = window_ref[...]
    rbuf[n_sta - 1] = sbuf[me]
    mbuf[n_sta - 1] = mrow[...]

    over_tpl(lambda peer: win_copy(peer, peer).wait_recv())

    lane_p = iota((8, LANES), 1)
    prior_tiles = prior_len // LANES
    prior_rest = prior_len % LANES

    for g in range(rows // 8):
        r8 = pl.ds(8 * g, 8)
        old = prior_ref[r8, :].astype(F32)
        new = jnp.concatenate(
            [win[p, r8, :].astype(F32) for p in range(n_tpl)] + [jnp.zeros((8, LANES), F32)], axis=1
        )
        new = pltpu.roll(new, prior_rest, 1)
        tail = jnp.concatenate(
            [old[:, prior_tiles * LANES :], jnp.zeros((8, LANES - prior_rest), F32)], axis=1
        )
        joint = jnp.where(lane_p < prior_rest, tail, new[:, :LANES])
        x = jnp.concatenate([old[:, : prior_tiles * LANES], joint, new[:, LANES:]], axis=1)
        for b in range(QUARTERS):
            moved_x = shift_left(x, SUB * b)
            for m in range(x_blocks):
                xs[b, pl.ds(pitch * 8 * g + m, 8, stride=pitch), :] = moved_x[
                    :, LANES * m : LANES * (m + 1)
                ]
        sums = {1: x * x}
        size = 1
        while 2 * size <= length:
            sums[2 * size] = sums[size] + shift_left(sums[size], size)
            size *= 2
        energy, done = None, 0
        while size:
            if length & size:
                part = shift_left(sums[size], done)
                energy = part if energy is None else energy + part
                done += size
            size //= 2
        scale = 1.0 / jnp.sqrt(energy[:, :lags] + EPSILON)
        for a in range(cells):
            sc[r8, a, :] = scale[:, LANES * a : LANES * (a + 1)]

    def build_row(c, _):
        for r in range(k_blocks):
            for b in range(0, QUARTERS, 2):
                pair = jnp.concatenate(
                    [xs[b + d, pl.ds(pitch * c + r, cells), :] for d in range(2)], axis=0
                )
                xall[c, pl.ds(cells * b, 2 * cells), pl.ds(LANES * r, LANES)] = pair.astype(BF16)
        return 0

    lax.fori_loop(0, rows, build_row, 0, unroll=4)

    quarter = iota((8, LANES), 1) // SUB

    def pick(parts):
        value = parts[0]
        for i in range(1, QUARTERS):
            value = jnp.where(quarter == i, parts[i], value)
        return value

    def correlate(s):
        wave = rbuf[s].astype(F32)
        codes = [msm[s, 0, cap * me + i] for i in range(cap)]
        local_rows = [code >> (group.bit_length() - 1) for code in codes]
        shifted = jnp.concatenate(
            [
                pltpu.roll(
                    jnp.broadcast_to(wave[i : i + 1], (SUB, k_width)), 0, 1, stride=1, stride_axis=0
                )
                for i in range(cap)
            ],
            axis=0,
        ).astype(BF16)
        data = jnp.concatenate([xall[c] for c in local_rows], axis=0)
        found = dot(data, shifted, NT)
        block = lambda i, b: found[SUB * i + cells * b : SUB * i + cells * (b + 1)]
        turned = []
        for d in range(QUARTERS):
            v = pick([block(i, (i + d) % QUARTERS) for i in range(cap)])
            turned.append(v if d == 0 else pltpu.roll(v, SUB * d, 1))
        out = []
        for i in range(cap):
            v = pick([turned[(b - i) % QUARTERS] for b in range(QUARTERS)])
            out.append(v * sc[local_rows[i]])
        traces = jnp.concatenate(out, axis=0)
        hi = traces.astype(BF16)
        lo = (traces - hi.astype(F32)).astype(BF16)
        here = pl.ds(cells * cap * s, cells * cap)
        ohl[here, pl.ds(0, LANES)] = hi
        ohl[here, pl.ds(LANES, LANES)] = lo

    def to_scalars(g):
        here = pl.ds(BATCH * g, BATCH)
        return pltpu.make_async_copy(mbuf.at[here], msm.at[here], sm_sem.at[g])

    def meta_here(g):
        here = batch_of(g)
        remote(mbuf.at[here], mbuf.at[here], meta_send, meta_recv.at[g], {"sta": me}).wait_recv()
        to_scalars(g).start()

    def waves_here(g):
        here = batch_of(g)
        remote(rbuf.at[here], rbuf.at[here], wave_send, wave_recv.at[g], {"sta": me}).wait_recv()

    meta_here(batches - 1)
    for g in reversed(range(batches)):
        if g:
            meta_here(g - 1)
        waves_here(g)
        to_scalars(g).wait()
        for k in range(BATCH):
            correlate(BATCH * g + k)

    codes = mbuf[...].reshape(n_sta, LANES)
    mine = pltpu.roll(codes, lax.rem(positions - cap * me, positions), 1)
    tmpl = mine & (group - 1)
    lane_s = iota((n_sta, LANES), 1)
    sub_s = iota((n_sta, LANES), 0)
    by_lane = jnp.zeros((n_sta, LANES), I32)
    for j in range(cap):
        by_lane = jnp.where(
            (lane_s // cells) % cap == j, jnp.broadcast_to(tmpl[:, j : j + 1], (n_sta, LANES)), by_lane
        )
    per_tile = LANES // (cap * cells)
    by_lane = by_lane.astype(F32)
    out_rows = group * cells
    row_t = (iota((out_rows, LANES), 0) // cells).astype(F32)
    same_a = iota((out_rows, LANES), 0) % cells == iota((out_rows, LANES), 1) % cells
    tiles = []
    for m in range(positions * cells // LANES):
        names = jnp.sum(
            jnp.where(sub_s == per_tile * m + lane_s // (cap * cells), by_lane, 0.0),
            axis=0,
            keepdims=True,
        )
        tiles.append(jnp.where((row_t == names) & same_a, 1.0, 0.0).astype(BF16))
    chooser = jnp.concatenate(tiles, axis=1)
    both = dot(chooser, ohl[...], NN)
    stacked = both[:, :LANES] + both[:, LANES:]
    for t in range(group):
        obuf[t] = stacked[cells * t : cells * (t + 1)]

    over_sta(lambda k, peer: res_copy(k, peer).start())
    rres[n_sta - 1] = obuf[me]
    others = pl.ds(0, n_sta - 1)
    over_tpl(lambda peer: win_copy(my_t, peer).wait_send())
    remote(mbuf.at[others], mbuf.at[others], meta_send, meta_recv.at[0], {"sta": me}).wait_send()
    remote(sbuf.at[others], sbuf.at[others], wave_send, wave_recv.at[0], {"sta": me}).wait_send()
    results = remote(obuf.at[others], rres.at[others], res_send, res_recv, {"sta": me})
    results.wait_send()
    results.wait_recv()
    total = jnp.sum(rres[...], axis=0)
    for a in range(cells):
        out_ref[0:1, pl.ds(LANES * a, LANES)] = total[a : a + 1]


def solution(mesh):
    n_sta, n_tpl = mesh.shape["sta"], mesh.shape["tpl"]

    def per_device(window, prior, waves, chan_list, chan_count, station_row):
        group, slots, length = waves.shape
        rows = window.shape[0]
        lags = window.shape[1] * n_tpl
        positions = group * slots
        cap = positions // n_sta
        cells = lags // LANES
        k_width = pl.cdiv(length + SUB - 1, LANES) * LANES
        cfg = (n_sta, n_tpl, group, slots, length, rows, lags, 8)
        vmem = pl.BlockSpec(memory_space=pltpu.VMEM)
        dma = pltpu.SemaphoreType.DMA
        return pl.pallas_call(
            functools.partial(kernel, cfg),
            out_shape=pltpu.VMEM((1, lags), F32),
            in_specs=[pl.BlockSpec(memory_space=pl.ANY)] * 6,
            out_specs=vmem,
            scratch_shapes=[
                pltpu.VMEM(window.shape, BF16),
                pltpu.VMEM(prior.shape, BF16),
                pltpu.VMEM(waves.shape, BF16),
                pltpu.VMEM((slots, group), I32),
                pltpu.VMEM((1, group), I32),
                pltpu.VMEM((1, station_row.shape[0]), I32),
                pltpu.VMEM((n_tpl, rows, window.shape[1]), BF16),
                pltpu.VMEM((k_width // LANES, positions, LANES), F32),
                pltpu.VMEM((n_sta, cap, k_width), BF16),
                pltpu.VMEM((n_sta, cap, k_width), BF16),
                pltpu.VMEM((1, positions), I32),
                pltpu.VMEM((n_sta, 1, positions), I32),
                pltpu.SMEM((n_sta, 1, positions), I32),
                pltpu.VMEM((QUARTERS, rows * pl.cdiv(length - 1 + lags, LANES), LANES), F32),
                pltpu.VMEM((rows, SUB, k_width), BF16),
                pltpu.VMEM((rows, cells, LANES), F32),
                pltpu.VMEM((positions * cells, 2 * LANES), BF16),
                pltpu.VMEM((group, cells, LANES), F32),
                pltpu.VMEM((n_sta, cells, LANES), F32),
                dma((n_tpl,)),
                dma((n_tpl,)),
                dma(()),
                dma((n_sta // BATCH,)),
                dma(()),
                dma((n_sta // BATCH,)),
                dma(()),
                dma(()),
                dma((n_sta // BATCH,)),
                dma((6,)),
            ],
            compiler_params=pltpu.CompilerParams(collective_id=0, has_side_effects=True),
        )(
            window,
            prior,
            waves,
            chan_list.T,
            chan_count.reshape(1, group),
            station_row.reshape(1, -1),
        )

    return jax.shard_map(
        per_device,
        mesh=mesh,
        in_specs=(
            P("sta", "tpl"),
            P("sta", None),
            P("tpl", "sta", None),
            P("tpl", "sta"),
            P("tpl"),
            P(),
        ),
        out_specs=P(("tpl", "sta"), None),
        check_vma=False,
    )
```

```python
import functools

import jax
import jax.numpy as jnp
from jax import lax
from jax.experimental import pallas as pl
from jax.experimental.pallas import tpu as pltpu
from jax.sharding import PartitionSpec as P

EPSILON = 1e-06
MESH = pl.DeviceIdType.MESH
F32 = jnp.float32
BF16 = jnp.bfloat16
I32 = jnp.int32
NT = (((1,), (1,)), ((), ()))
NN = (((1,), (0,)), ((), ()))

LANES = 128
SUB = 32
BATCH = 8
PACK = 16
QUARTERS = LANES // SUB


def iota(shape, dim):
    return lax.broadcasted_iota(I32, shape, dim)


def dot(a, b, dims):
    return lax.dot_general(a, b, dims, preferred_element_type=F32)


def shift_left(v, n):
    width = v.shape[1]
    return v if n == 0 else pltpu.roll(v, width - n, 1)


def kernel(
    cfg,
    window_hbm,
    prior_hbm,
    waves_hbm,
    chan_hbm,
    count_hbm,
    table_hbm,
    out_ref,
    window_ref,
    prior_ref,
    waves_ref,
    chan_ref,
    count_ref,
    table_ref,
    win,
    flat,
    sbuf,
    rbuf,
    band,
    squares,
    mrow,
    mbuf,
    msm,
    xs,
    xall,
    sc,
    ohl,
    obuf,
    rres,
    win_send,
    win_recv,
    wave_send,
    wave_recv,
    meta_send,
    meta_recv,
    res_send,
    res_recv,
    sm_sem,
    in_sem,
):
    n_sta, n_tpl, group, slots, length, rows, lags, z_size = cfg
    positions = group * slots
    prior_len = length - 1
    cells = lags // LANES
    k_blocks = pl.cdiv(length + SUB - 1, LANES)
    k_width = k_blocks * LANES
    x_blocks = pl.cdiv(prior_len + lags, LANES)
    pitch = x_blocks
    me = lax.axis_index("sta")
    my_t = lax.axis_index("tpl")

    y_size = n_sta // z_size
    my_y = lax.div(me, z_size)
    my_z = me - my_y * z_size

    def outward(n):
        return sorted(range(n), key=lambda d: -min(d, n - d))

    at_z = [lax.rem(my_z + d, z_size) for d in outward(z_size)]
    at_y = [lax.rem(my_y + d, y_size) * z_size for d in outward(y_size)]
    peers = [z + y for z in at_z for y in at_y][: n_sta - 1]
    tpl_peers = [lax.rem(my_t + o, n_tpl) for o in range(1, n_tpl)]

    barrier = pltpu.get_barrier_semaphore()

    for peer in peers:
        pl.semaphore_signal(barrier, inc=1, device_id={"sta": peer}, device_id_type=MESH)
    for peer in tpl_peers:
        pl.semaphore_signal(barrier, inc=1, device_id={"tpl": peer}, device_id_type=MESH)
    inputs = [
        pltpu.make_async_copy(src, dst, in_sem.at[n])
        for n, (src, dst) in enumerate(
            [
                (chan_hbm, chan_ref),
                (count_hbm, count_ref),
                (table_hbm, table_ref),
                (waves_hbm, waves_ref),
                (window_hbm, window_ref),
                (prior_hbm, prior_ref),
            ]
        )
    ]
    for copy in inputs:
        copy.start()
    for copy in inputs:
        copy.wait()

    square = (positions, positions)
    lane = iota(square, 1)
    sub = iota(square, 0)
    lane1 = iota((1, positions), 1)
    template = lane1 % group

    def to_rows(row):
        return jnp.broadcast_to(row, square).T

    chan = jnp.concatenate([chan_ref[j : j + 1, :] for j in range(slots)], axis=1)
    counts = jnp.concatenate([count_ref[...]] * slots, axis=1)
    station = (chan * 43691) >> 17
    station_rows = to_rows(station)
    looked = jnp.zeros(square, I32)
    for h in range(table_ref.shape[1] // LANES):
        entries = jnp.broadcast_to(table_ref[:, pl.ds(LANES * h, LANES)], square)
        looked = jnp.where(station_rows == lane + LANES * h, entries, looked)
    looked = jnp.sum(looked.T, axis=0, keepdims=True)
    block_stations = rows // 3
    owner = looked // block_stations
    local = 3 * (looked % block_stations) + chan - 3 * station
    cap = positions // n_sta
    before = (to_rows(owner) == owner) & (sub < lane)
    rank = jnp.sum(jnp.where(before, 1, 0), axis=0, keepdims=True)
    slot_at = owner * cap + rank
    place = sub == slot_at
    listed = jnp.where(me * slots + lane1 // group < counts, 1.0, 0.0)
    code_rows = to_rows(local * group + template)
    mrow[...] = jnp.sum(jnp.where(to_rows(slot_at) == lane, code_rows, 0), axis=0, keepdims=True)

    for t in range(0, group):
        wave = waves_ref[t].astype(F32)
        wave = jnp.concatenate([wave, jnp.zeros((slots, k_width - length), F32)], axis=1)
        for r in range(k_blocks):
            flat[r, pl.ds(t, slots, stride=group), :] = wave[:, LANES * r : LANES * (r + 1)]
    mover = jnp.where(place, jnp.broadcast_to(listed, (positions, positions)), 0.0).astype(BF16)
    moved = jnp.concatenate(
        [dot(mover, flat[r].astype(BF16), NN) for r in range(k_blocks)], axis=1
    )
    norms = jnp.sqrt(jnp.sum(moved * moved, axis=1, keepdims=True) + EPSILON)
    normed = moved / norms
    for s in range(n_sta):
        sbuf[s] = normed[cap * s : cap * (s + 1)].astype(BF16)

    e_width = pl.cdiv(length + LANES - 1, LANES) * LANES
    ahead = iota((e_width, LANES), 0) - iota((e_width, LANES), 1)
    band[...] = jnp.where((ahead >= 0) & (ahead < length), 1.0, 0.0).astype(BF16)

    pl.semaphore_wait(barrier, n_sta + n_tpl - 2)

    def remote(src, dst, send, recv, device):
        return pltpu.make_async_remote_copy(
            src_ref=src,
            dst_ref=dst,
            send_sem=send,
            recv_sem=recv,
            device_id=device,
            device_id_type=MESH,
        )

    def win_copy(slot, peer):
        return remote(window_ref, win.at[slot], win_send.at[peer], win_recv.at[slot], {"tpl": peer})

    def wave_copy(k, peer):
        return remote(
            sbuf.at[peer], rbuf.at[k], wave_send, wave_recv.at[k // BATCH], {"sta": peer}
        )

    def meta_copy(k, peer):
        return remote(
            mrow, mbuf.at[k], meta_send, meta_recv.at[k // BATCH], {"sta": peer}
        )

    def res_copy(k, peer):
        return remote(obuf.at[peer], rres.at[k], res_send, res_recv, {"sta": peer})

    def over_tpl(body):
        for peer in tpl_peers:
            body(peer)

    def over_sta(body):
        for k, peer in enumerate(peers):
            body(k, peer)

    batches = n_sta // BATCH

    def batch_of(g):
        return pl.ds(BATCH * g, BATCH - 1 if g == batches - 1 else BATCH)

    over_tpl(lambda peer: win_copy(my_t, peer).start())
    over_sta(lambda k, peer: meta_copy(k, peer).start())
    over_sta(lambda k, peer: wave_copy(k, peer).start())
    win[my_t] = window_ref[...]
    rbuf[n_sta - 1] = sbuf[me]
    mbuf[n_sta - 1] = mrow[...]

    quarter = iota((8, LANES), 1) // SUB

    def pick(parts):
        value = parts[0]
        for i in range(1, QUARTERS):
            value = jnp.where(quarter == i, parts[i], value)
        return value

    def shift_waves(s):
        wave = rbuf[s].astype(F32)
        return jnp.concatenate(
            [
                pltpu.roll(
                    jnp.broadcast_to(wave[i : i + 1], (SUB, k_width)), 0, 1, stride=1, stride_axis=0
                )
                for i in range(cap)
            ],
            axis=0,
        ).astype(BF16)

    def correlate(s, shifted):
        codes = [msm[s, 0, cap * me + i] for i in range(cap)]
        local_rows = [code >> (group.bit_length() - 1) for code in codes]
        data = jnp.concatenate([xall[c] for c in local_rows], axis=0)
        found = dot(data, shifted, NT)
        block = lambda i, b: found[SUB * i + cells * b : SUB * i + cells * (b + 1)]
        turned = []
        for d in range(QUARTERS):
            v = pick([block(i, (i + d) % QUARTERS) for i in range(cap)])
            turned.append(v if d == 0 else pltpu.roll(v, SUB * d, 1))
        out = []
        for i in range(cap):
            v = pick([turned[(b - i) % QUARTERS] for b in range(QUARTERS)])
            out.append(v * sc[local_rows[i]])
        traces = jnp.concatenate(out, axis=0)
        hi = traces.astype(BF16)
        lo = (traces - hi.astype(F32)).astype(BF16)
        here = pl.ds(cells * cap * s, cells * cap)
        ohl[here, pl.ds(0, LANES)] = hi
        ohl[here, pl.ds(LANES, LANES)] = lo

    def to_scalars(g):
        here = pl.ds(BATCH * g, BATCH)
        return pltpu.make_async_copy(mbuf.at[here], msm.at[here], sm_sem.at[g])

    def meta_here(g):
        here = batch_of(g)
        remote(mbuf.at[here], mbuf.at[here], meta_send, meta_recv.at[g], {"sta": me}).wait_recv()
        to_scalars(g).start()

    def waves_here(g):
        here = batch_of(g)
        remote(rbuf.at[here], rbuf.at[here], wave_send, wave_recv.at[g], {"sta": me}).wait_recv()

    first = batches - 1
    meta_here(first)
    over_tpl(lambda peer: win_copy(peer, peer).wait_recv())

    lane_p = iota((PACK, LANES), 1)
    prior_tiles = prior_len // LANES
    prior_rest = prior_len % LANES

    for g in range(rows // PACK):
        here = pl.ds(PACK * g, PACK)
        old = prior_ref[here, :].astype(F32)
        new = jnp.concatenate(
            [win[p, here, :].astype(F32) for p in range(n_tpl)] + [jnp.zeros((PACK, LANES), F32)],
            axis=1,
        )
        new = pltpu.roll(new, prior_rest, 1)
        tail = jnp.concatenate(
            [old[:, prior_tiles * LANES :], jnp.zeros((PACK, LANES - prior_rest), F32)], axis=1
        )
        joint = jnp.where(lane_p < prior_rest, tail, new[:, :LANES])
        x = jnp.concatenate([old[:, : prior_tiles * LANES], joint, new[:, LANES:]], axis=1)
        for b in range(QUARTERS):
            moved_x = shift_left(x, SUB * b)
            for m in range(x_blocks):
                xs[b, pl.ds(pitch * PACK * g + m, PACK, stride=pitch), :] = moved_x[
                    :, LANES * m : LANES * (m + 1)
                ]
        square = x * x
        high = square.astype(BF16)
        squares[here, :] = high
        squares[pl.ds(rows + PACK * g, PACK), :] = (square - high.astype(F32)).astype(BF16)

    energy = dot(
        jnp.concatenate([squares[:, pl.ds(LANES * a, e_width)] for a in range(cells)], axis=0),
        band[...],
        NN,
    )
    for a in range(cells):
        high_part = energy[2 * rows * a : 2 * rows * a + rows]
        low_part = energy[2 * rows * a + rows : 2 * rows * (a + 1)]
        sc[:, a, :] = 1.0 / jnp.sqrt(high_part + low_part + EPSILON)

    def build_row(c, _):
        for r in range(k_blocks):
            for b in range(0, QUARTERS, 2):
                pair = jnp.concatenate(
                    [xs[b + d, pl.ds(pitch * c + r, cells), :] for d in range(2)], axis=0
                )
                xall[c, pl.ds(cells * b, 2 * cells), pl.ds(LANES * r, LANES)] = pair.astype(BF16)
        return 0

    lax.fori_loop(0, rows, build_row, 0, unroll=4)

    for g in reversed(range(batches)):
        if g:
            meta_here(g - 1)
        waves_here(g)
        to_scalars(g).wait()
        for k in range(BATCH):
            correlate(BATCH * g + k, shift_waves(BATCH * g + k))

    codes = mbuf[...].reshape(n_sta, LANES)
    mine = pltpu.roll(codes, lax.rem(positions - cap * me, positions), 1)
    tmpl = mine & (group - 1)
    lane_s = iota((n_sta, LANES), 1)
    sub_s = iota((n_sta, LANES), 0)
    by_lane = jnp.zeros((n_sta, LANES), I32)
    for j in range(cap):
        by_lane = jnp.where(
            (lane_s // cells) % cap == j, jnp.broadcast_to(tmpl[:, j : j + 1], (n_sta, LANES)), by_lane
        )
    per_tile = LANES // (cap * cells)
    by_lane = by_lane.astype(F32)
    out_rows = group * cells
    row_t = (iota((out_rows, LANES), 0) // cells).astype(F32)
    same_a = iota((out_rows, LANES), 0) % cells == iota((out_rows, LANES), 1) % cells
    tiles = []
    for m in range(positions * cells // LANES):
        names = jnp.sum(
            jnp.where(sub_s == per_tile * m + lane_s // (cap * cells), by_lane, 0.0),
            axis=0,
            keepdims=True,
        )
        tiles.append(jnp.where((row_t == names) & same_a, 1.0, 0.0).astype(BF16))
    chooser = jnp.concatenate(tiles, axis=1)
    both = dot(chooser, ohl[...], NN)
    stacked = both[:, :LANES] + both[:, LANES:]
    for t in range(group):
        obuf[t] = stacked[cells * t : cells * (t + 1)]

    over_sta(lambda k, peer: res_copy(k, peer).start())
    rres[n_sta - 1] = obuf[me]
    others = pl.ds(0, n_sta - 1)
    over_tpl(lambda peer: win_copy(my_t, peer).wait_send())
    remote(mbuf.at[others], mbuf.at[others], meta_send, meta_recv.at[0], {"sta": me}).wait_send()
    remote(sbuf.at[others], sbuf.at[others], wave_send, wave_recv.at[0], {"sta": me}).wait_send()
    results = remote(obuf.at[others], rres.at[others], res_send, res_recv, {"sta": me})
    results.wait_send()
    results.wait_recv()
    total = jnp.sum(rres[...], axis=0)
    for a in range(cells):
        out_ref[0:1, pl.ds(LANES * a, LANES)] = total[a : a + 1]


def solution(mesh):
    n_sta, n_tpl = mesh.shape["sta"], mesh.shape["tpl"]

    def per_device(window, prior, waves, chan_list, chan_count, station_row):
        group, slots, length = waves.shape
        rows = window.shape[0]
        lags = window.shape[1] * n_tpl
        positions = group * slots
        cap = positions // n_sta
        cells = lags // LANES
        k_width = pl.cdiv(length + SUB - 1, LANES) * LANES
        cfg = (n_sta, n_tpl, group, slots, length, rows, lags, 8)
        vmem = pl.BlockSpec(memory_space=pltpu.VMEM)
        dma = pltpu.SemaphoreType.DMA
        return pl.pallas_call(
            functools.partial(kernel, cfg),
            out_shape=pltpu.VMEM((1, lags), F32),
            in_specs=[pl.BlockSpec(memory_space=pl.ANY)] * 6,
            out_specs=vmem,
            scratch_shapes=[
                pltpu.VMEM(window.shape, BF16),
                pltpu.VMEM(prior.shape, BF16),
                pltpu.VMEM(waves.shape, BF16),
                pltpu.VMEM((slots, group), I32),
                pltpu.VMEM((1, group), I32),
                pltpu.VMEM((1, station_row.shape[0]), I32),
                pltpu.VMEM((n_tpl, rows, window.shape[1]), BF16),
                pltpu.VMEM((k_width // LANES, positions, LANES), F32),
                pltpu.VMEM((n_sta, cap, k_width), BF16),
                pltpu.VMEM((n_sta, cap, k_width), BF16),
                pltpu.VMEM((pl.cdiv(length + LANES - 1, LANES) * LANES, LANES), BF16),
                pltpu.VMEM((2 * rows, pl.cdiv(length - 1 + lags, LANES) * LANES), BF16),
                pltpu.VMEM((1, positions), I32),
                pltpu.VMEM((n_sta, 1, positions), I32),
                pltpu.SMEM((n_sta, 1, positions), I32),
                pltpu.VMEM((QUARTERS, rows * pl.cdiv(length - 1 + lags, LANES), LANES), F32),
                pltpu.VMEM((rows, SUB, k_width), BF16),
                pltpu.VMEM((rows, cells, LANES), F32),
                pltpu.VMEM((positions * cells, 2 * LANES), BF16),
                pltpu.VMEM((group, cells, LANES), F32),
                pltpu.VMEM((n_sta, cells, LANES), F32),
                dma((n_tpl,)),
                dma((n_tpl,)),
                dma(()),
                dma((n_sta // BATCH,)),
                dma(()),
                dma((n_sta // BATCH,)),
                dma(()),
                dma(()),
                dma((n_sta // BATCH,)),
                dma((6,)),
            ],
            compiler_params=pltpu.CompilerParams(collective_id=0, has_side_effects=True),
        )(
            window,
            prior,
            waves,
            chan_list.T,
            chan_count.reshape(1, group),
            station_row.reshape(1, -1),
        )

    return jax.shard_map(
        per_device,
        mesh=mesh,
        in_specs=(
            P("sta", "tpl"),
            P("sta", None),
            P("tpl", "sta", None),
            P("tpl", "sta"),
            P("tpl"),
            P(),
        ),
        out_specs=P(("tpl", "sta"), None),
        check_vma=False,
    )
```

```python
import functools

import jax
import jax.numpy as jnp
from jax import lax
from jax.experimental import pallas as pl
from jax.experimental.pallas import tpu as pltpu
from jax.sharding import PartitionSpec as P

EPSILON = 1e-06
MESH = pl.DeviceIdType.MESH
F32 = jnp.float32
BF16 = jnp.bfloat16
I32 = jnp.int32
NT = (((1,), (1,)), ((), ()))
NN = (((1,), (0,)), ((), ()))

LANES = 128
SUB = 32
BATCH = 8
PACK = 16
QUARTERS = LANES // SUB


def iota(shape, dim):
    return lax.broadcasted_iota(I32, shape, dim)


def dot(a, b, dims):
    return lax.dot_general(a, b, dims, preferred_element_type=F32)


def shift_left(v, n):
    width = v.shape[1]
    return v if n == 0 else pltpu.roll(v, width - n, 1)


def kernel(
    cfg,
    window_hbm,
    prior_hbm,
    waves_hbm,
    chan_hbm,
    count_hbm,
    table_hbm,
    out_ref,
    window_ref,
    prior_ref,
    waves_ref,
    chan_ref,
    count_ref,
    table_ref,
    win,
    flat,
    sbuf,
    rbuf,
    band,
    squares,
    mrow,
    mbuf,
    msm,
    xs,
    xall,
    sc,
    ohl,
    obuf,
    rres,
    win_send,
    win_recv,
    wave_send,
    wave_recv,
    meta_send,
    meta_recv,
    res_send,
    res_recv,
    sm_sem,
    in_sem,
):
    n_sta, n_tpl, group, slots, length, rows, lags, z_size = cfg
    positions = group * slots
    prior_len = length - 1
    cells = lags // LANES
    k_blocks = pl.cdiv(length + SUB - 1, LANES)
    k_width = k_blocks * LANES
    x_blocks = pl.cdiv(prior_len + lags, LANES)
    pitch = x_blocks
    me = lax.axis_index("sta")
    my_t = lax.axis_index("tpl")

    y_size = n_sta // z_size
    my_y = lax.div(me, z_size)
    my_z = me - my_y * z_size

    def outward(n):
        return sorted(range(n), key=lambda d: -min(d, n - d))

    at_z = [lax.rem(my_z + d, z_size) for d in outward(z_size)]
    at_y = [lax.rem(my_y + d, y_size) * z_size for d in outward(y_size)]
    peers = [z + y for z in at_z for y in at_y][: n_sta - 1]
    tpl_peers = [lax.rem(my_t + o, n_tpl) for o in range(1, n_tpl)]

    barrier = pltpu.get_barrier_semaphore()

    for peer in peers:
        pl.semaphore_signal(barrier, inc=1, device_id={"sta": peer}, device_id_type=MESH)
    for peer in tpl_peers:
        pl.semaphore_signal(barrier, inc=1, device_id={"tpl": peer}, device_id_type=MESH)
    inputs = [
        pltpu.make_async_copy(src, dst, in_sem.at[n])
        for n, (src, dst) in enumerate(
            [
                (chan_hbm, chan_ref),
                (count_hbm, count_ref),
                (table_hbm, table_ref),
                (waves_hbm, waves_ref),
                (window_hbm, window_ref),
                (prior_hbm, prior_ref),
            ]
        )
    ]
    for copy in inputs:
        copy.start()
    for copy in inputs:
        copy.wait()

    square = (positions, positions)
    lane = iota(square, 1)
    sub = iota(square, 0)
    lane1 = iota((1, positions), 1)
    template = lane1 % group

    def to_rows(row):
        return jnp.broadcast_to(row, square).T

    chan = jnp.concatenate([chan_ref[j : j + 1, :] for j in range(slots)], axis=1)
    counts = jnp.concatenate([count_ref[...]] * slots, axis=1)
    station = (chan * 43691) >> 17
    station_rows = to_rows(station)
    looked = jnp.zeros(square, I32)
    for h in range(table_ref.shape[1] // LANES):
        entries = jnp.broadcast_to(table_ref[:, pl.ds(LANES * h, LANES)], square)
        looked = jnp.where(station_rows == lane + LANES * h, entries, looked)
    looked = jnp.sum(looked.T, axis=0, keepdims=True)
    block_stations = rows // 3
    owner = looked // block_stations
    local = 3 * (looked % block_stations) + chan - 3 * station
    cap = positions // n_sta
    before = (to_rows(owner) == owner) & (sub < lane)
    rank = jnp.sum(jnp.where(before, 1, 0), axis=0, keepdims=True)
    slot_at = owner * cap + rank
    place = sub == slot_at
    listed = jnp.where(me * slots + lane1 // group < counts, 1.0, 0.0)
    code_rows = to_rows(local * group + template)
    mrow[...] = jnp.sum(jnp.where(to_rows(slot_at) == lane, code_rows, 0), axis=0, keepdims=True)

    for t in range(0, group):
        wave = waves_ref[t].astype(F32)
        wave = jnp.concatenate([wave, jnp.zeros((slots, k_width - length), F32)], axis=1)
        for r in range(k_blocks):
            flat[r, pl.ds(t, slots, stride=group), :] = wave[:, LANES * r : LANES * (r + 1)]
    mover = jnp.where(place, jnp.broadcast_to(listed, (positions, positions)), 0.0).astype(BF16)
    moved = jnp.concatenate(
        [dot(mover, flat[r].astype(BF16), NN) for r in range(k_blocks)], axis=1
    )
    norms = jnp.sqrt(jnp.sum(moved * moved, axis=1, keepdims=True) + EPSILON)
    normed = moved / norms
    for s in range(n_sta):
        sbuf[s] = normed[cap * s : cap * (s + 1)].astype(BF16)

    e_width = pl.cdiv(length + LANES - 1, LANES) * LANES
    ahead = iota((e_width, LANES), 0) - iota((e_width, LANES), 1)
    band[...] = jnp.where((ahead >= 0) & (ahead < length), 1.0, 0.0).astype(BF16)

    pl.semaphore_wait(barrier, n_sta + n_tpl - 2)

    def remote(src, dst, send, recv, device):
        return pltpu.make_async_remote_copy(
            src_ref=src,
            dst_ref=dst,
            send_sem=send,
            recv_sem=recv,
            device_id=device,
            device_id_type=MESH,
        )

    def win_copy(slot, peer):
        return remote(window_ref, win.at[slot], win_send.at[peer], win_recv.at[slot], {"tpl": peer})

    def wave_copy(k, peer):
        return remote(
            sbuf.at[peer], rbuf.at[k], wave_send, wave_recv.at[k // BATCH], {"sta": peer}
        )

    def meta_copy(k, peer):
        return remote(
            mrow, mbuf.at[k], meta_send, meta_recv.at[k // BATCH], {"sta": peer}
        )

    def res_copy(k, peer):
        return remote(obuf.at[peer], rres.at[k], res_send, res_recv, {"sta": peer})

    def over_tpl(body):
        for peer in tpl_peers:
            body(peer)

    def over_sta(body):
        for k, peer in enumerate(peers):
            body(k, peer)

    batches = n_sta // BATCH

    def batch_of(g):
        return pl.ds(BATCH * g, BATCH - 1 if g == batches - 1 else BATCH)

    over_tpl(lambda peer: win_copy(my_t, peer).start())
    for k, peer in reversed(list(enumerate(peers))):
        meta_copy(k, peer).start()
    for k, peer in reversed(list(enumerate(peers))):
        wave_copy(k, peer).start()
    win[my_t] = window_ref[...]
    rbuf[n_sta - 1] = sbuf[me]
    mbuf[n_sta - 1] = mrow[...]

    quarter = iota((8, LANES), 1) // SUB

    def pick(parts):
        value = parts[0]
        for i in range(1, QUARTERS):
            value = jnp.where(quarter == i, parts[i], value)
        return value

    def shift_waves(s):
        wave = rbuf[s].astype(F32)
        return jnp.concatenate(
            [
                pltpu.roll(
                    jnp.broadcast_to(wave[i : i + 1], (SUB, k_width)), 0, 1, stride=1, stride_axis=0
                )
                for i in range(cap)
            ],
            axis=0,
        ).astype(BF16)

    def correlate(s, shifted):
        codes = [msm[s, 0, cap * me + i] for i in range(cap)]
        local_rows = [code >> (group.bit_length() - 1) for code in codes]
        data = jnp.concatenate([xall[c] for c in local_rows], axis=0)
        found = dot(data, shifted, NT)
        block = lambda i, b: found[SUB * i + cells * b : SUB * i + cells * (b + 1)]
        turned = []
        for d in range(QUARTERS):
            v = pick([block(i, (i + d) % QUARTERS) for i in range(cap)])
            turned.append(v if d == 0 else pltpu.roll(v, SUB * d, 1))
        out = []
        for i in range(cap):
            v = pick([turned[(b - i) % QUARTERS] for b in range(QUARTERS)])
            out.append(v * sc[local_rows[i]])
        traces = jnp.concatenate(out, axis=0)
        hi = traces.astype(BF16)
        lo = (traces - hi.astype(F32)).astype(BF16)
        here = pl.ds(cells * cap * s, cells * cap)
        ohl[here, pl.ds(0, LANES)] = hi
        ohl[here, pl.ds(LANES, LANES)] = lo

    def to_scalars(g):
        here = pl.ds(BATCH * g, BATCH)
        return pltpu.make_async_copy(mbuf.at[here], msm.at[here], sm_sem.at[g])

    def meta_here(g):
        here = batch_of(g)
        remote(mbuf.at[here], mbuf.at[here], meta_send, meta_recv.at[g], {"sta": me}).wait_recv()
        to_scalars(g).start()

    def waves_here(g):
        here = batch_of(g)
        remote(rbuf.at[here], rbuf.at[here], wave_send, wave_recv.at[g], {"sta": me}).wait_recv()

    first = batches - 1
    meta_here(first)
    over_tpl(lambda peer: win_copy(peer, peer).wait_recv())

    lane_p = iota((PACK, LANES), 1)
    prior_tiles = prior_len // LANES
    prior_rest = prior_len % LANES

    for g in range(rows // PACK):
        here = pl.ds(PACK * g, PACK)
        old = prior_ref[here, :].astype(F32)
        new = jnp.concatenate(
            [win[p, here, :].astype(F32) for p in range(n_tpl)] + [jnp.zeros((PACK, LANES), F32)],
            axis=1,
        )
        new = pltpu.roll(new, prior_rest, 1)
        tail = jnp.concatenate(
            [old[:, prior_tiles * LANES :], jnp.zeros((PACK, LANES - prior_rest), F32)], axis=1
        )
        joint = jnp.where(lane_p < prior_rest, tail, new[:, :LANES])
        x = jnp.concatenate([old[:, : prior_tiles * LANES], joint, new[:, LANES:]], axis=1)
        for b in range(QUARTERS):
            moved_x = shift_left(x, SUB * b)
            for m in range(x_blocks):
                xs[b, pl.ds(pitch * PACK * g + m, PACK, stride=pitch), :] = moved_x[
                    :, LANES * m : LANES * (m + 1)
                ]
        square = x * x
        high = square.astype(BF16)
        squares[here, :] = high
        squares[pl.ds(rows + PACK * g, PACK), :] = (square - high.astype(F32)).astype(BF16)

    energy = dot(
        jnp.concatenate([squares[:, pl.ds(LANES * a, e_width)] for a in range(cells)], axis=0),
        band[...],
        NN,
    )
    for a in range(cells):
        high_part = energy[2 * rows * a : 2 * rows * a + rows]
        low_part = energy[2 * rows * a + rows : 2 * rows * (a + 1)]
        sc[:, a, :] = 1.0 / jnp.sqrt(high_part + low_part + EPSILON)

    def build_row(c, _):
        for r in range(k_blocks):
            for b in range(0, QUARTERS, 2):
                pair = jnp.concatenate(
                    [xs[b + d, pl.ds(pitch * c + r, cells), :] for d in range(2)], axis=0
                )
                xall[c, pl.ds(cells * b, 2 * cells), pl.ds(LANES * r, LANES)] = pair.astype(BF16)
        return 0

    lax.fori_loop(0, rows, build_row, 0, unroll=4)

    for g in reversed(range(batches)):
        if g:
            meta_here(g - 1)
        waves_here(g)
        to_scalars(g).wait()
        for k in range(BATCH):
            correlate(BATCH * g + k, shift_waves(BATCH * g + k))

    codes = mbuf[...].reshape(n_sta, LANES)
    mine = pltpu.roll(codes, lax.rem(positions - cap * me, positions), 1)
    tmpl = mine & (group - 1)
    lane_s = iota((n_sta, LANES), 1)
    sub_s = iota((n_sta, LANES), 0)
    by_lane = jnp.zeros((n_sta, LANES), I32)
    for j in range(cap):
        by_lane = jnp.where(
            (lane_s // cells) % cap == j, jnp.broadcast_to(tmpl[:, j : j + 1], (n_sta, LANES)), by_lane
        )
    per_tile = LANES // (cap * cells)
    by_lane = by_lane.astype(F32)
    out_rows = group * cells
    row_t = (iota((out_rows, LANES), 0) // cells).astype(F32)
    same_a = iota((out_rows, LANES), 0) % cells == iota((out_rows, LANES), 1) % cells
    tiles = []
    for m in range(positions * cells // LANES):
        names = jnp.sum(
            jnp.where(sub_s == per_tile * m + lane_s // (cap * cells), by_lane, 0.0),
            axis=0,
            keepdims=True,
        )
        tiles.append(jnp.where((row_t == names) & same_a, 1.0, 0.0).astype(BF16))
    chooser = jnp.concatenate(tiles, axis=1)
    both = dot(chooser, ohl[...], NN)
    stacked = both[:, :LANES] + both[:, LANES:]
    for t in range(group):
        obuf[t] = stacked[cells * t : cells * (t + 1)]

    over_sta(lambda k, peer: res_copy(k, peer).start())
    rres[n_sta - 1] = obuf[me]
    others = pl.ds(0, n_sta - 1)
    over_tpl(lambda peer: win_copy(my_t, peer).wait_send())
    remote(mbuf.at[others], mbuf.at[others], meta_send, meta_recv.at[0], {"sta": me}).wait_send()
    remote(sbuf.at[others], sbuf.at[others], wave_send, wave_recv.at[0], {"sta": me}).wait_send()
    results = remote(obuf.at[others], rres.at[others], res_send, res_recv, {"sta": me})
    results.wait_send()
    results.wait_recv()
    total = jnp.sum(rres[...], axis=0)
    for a in range(cells):
        out_ref[0:1, pl.ds(LANES * a, LANES)] = total[a : a + 1]


def solution(mesh):
    n_sta, n_tpl = mesh.shape["sta"], mesh.shape["tpl"]

    def per_device(window, prior, waves, chan_list, chan_count, station_row):
        group, slots, length = waves.shape
        rows = window.shape[0]
        lags = window.shape[1] * n_tpl
        positions = group * slots
        cap = positions // n_sta
        cells = lags // LANES
        k_width = pl.cdiv(length + SUB - 1, LANES) * LANES
        cfg = (n_sta, n_tpl, group, slots, length, rows, lags, 8)
        vmem = pl.BlockSpec(memory_space=pltpu.VMEM)
        dma = pltpu.SemaphoreType.DMA
        return pl.pallas_call(
            functools.partial(kernel, cfg),
            out_shape=pltpu.VMEM((1, lags), F32),
            in_specs=[pl.BlockSpec(memory_space=pl.ANY)] * 6,
            out_specs=vmem,
            scratch_shapes=[
                pltpu.VMEM(window.shape, BF16),
                pltpu.VMEM(prior.shape, BF16),
                pltpu.VMEM(waves.shape, BF16),
                pltpu.VMEM((slots, group), I32),
                pltpu.VMEM((1, group), I32),
                pltpu.VMEM((1, station_row.shape[0]), I32),
                pltpu.VMEM((n_tpl, rows, window.shape[1]), BF16),
                pltpu.VMEM((k_width // LANES, positions, LANES), F32),
                pltpu.VMEM((n_sta, cap, k_width), BF16),
                pltpu.VMEM((n_sta, cap, k_width), BF16),
                pltpu.VMEM((pl.cdiv(length + LANES - 1, LANES) * LANES, LANES), BF16),
                pltpu.VMEM((2 * rows, pl.cdiv(length - 1 + lags, LANES) * LANES), BF16),
                pltpu.VMEM((1, positions), I32),
                pltpu.VMEM((n_sta, 1, positions), I32),
                pltpu.SMEM((n_sta, 1, positions), I32),
                pltpu.VMEM((QUARTERS, rows * pl.cdiv(length - 1 + lags, LANES), LANES), F32),
                pltpu.VMEM((rows, SUB, k_width), BF16),
                pltpu.VMEM((rows, cells, LANES), F32),
                pltpu.VMEM((positions * cells, 2 * LANES), BF16),
                pltpu.VMEM((group, cells, LANES), F32),
                pltpu.VMEM((n_sta, cells, LANES), F32),
                dma((n_tpl,)),
                dma((n_tpl,)),
                dma(()),
                dma((n_sta // BATCH,)),
                dma(()),
                dma((n_sta // BATCH,)),
                dma(()),
                dma(()),
                dma((n_sta // BATCH,)),
                dma((6,)),
            ],
            compiler_params=pltpu.CompilerParams(collective_id=0, has_side_effects=True),
        )(
            window,
            prior,
            waves,
            chan_list.T,
            chan_count.reshape(1, group),
            station_row.reshape(1, -1),
        )

    return jax.shard_map(
        per_device,
        mesh=mesh,
        in_specs=(
            P("sta", "tpl"),
            P("sta", None),
            P("tpl", "sta", None),
            P("tpl", "sta"),
            P("tpl"),
            P(),
        ),
        out_specs=P(("tpl", "sta"), None),
        check_vma=False,
    )
```

```python
import functools

import jax
import jax.numpy as jnp
from jax import lax
from jax.experimental import pallas as pl
from jax.experimental.pallas import tpu as pltpu
from jax.sharding import PartitionSpec as P

EPSILON = 1e-06
MESH = pl.DeviceIdType.MESH
F32 = jnp.float32
BF16 = jnp.bfloat16
I32 = jnp.int32
NT = (((1,), (1,)), ((), ()))
NN = (((1,), (0,)), ((), ()))

LANES = 128
SUB = 32
BATCH = 8
PACK = 16
QUARTERS = LANES // SUB


def iota(shape, dim):
    return lax.broadcasted_iota(I32, shape, dim)


def dot(a, b, dims):
    return lax.dot_general(a, b, dims, preferred_element_type=F32)


def shift_left(v, n):
    width = v.shape[1]
    return v if n == 0 else pltpu.roll(v, width - n, 1)


def kernel(
    cfg,
    window_hbm,
    prior_hbm,
    waves_hbm,
    chan_hbm,
    count_hbm,
    table_hbm,
    out_ref,
    window_ref,
    prior_ref,
    waves_ref,
    chan_ref,
    count_ref,
    table_ref,
    win,
    flat,
    sbuf,
    rbuf,
    band,
    squares,
    mrow,
    mbuf,
    msm,
    xs,
    xall,
    sc,
    ohl,
    obuf,
    rres,
    win_send,
    win_recv,
    wave_send,
    wave_recv,
    meta_send,
    meta_recv,
    res_send,
    res_recv,
    sm_sem,
    in_sem,
):
    n_sta, n_tpl, group, slots, length, rows, lags, z_size = cfg
    positions = group * slots
    prior_len = length - 1
    cells = lags // LANES
    k_blocks = pl.cdiv(length + SUB - 1, LANES)
    k_width = k_blocks * LANES
    x_blocks = pl.cdiv(prior_len + lags, LANES)
    pitch = x_blocks
    me = lax.axis_index("sta")
    my_t = lax.axis_index("tpl")

    y_size = n_sta // z_size
    my_y = lax.div(me, z_size)
    my_z = me - my_y * z_size

    def outward(n):
        return sorted(range(n), key=lambda d: -min(d, n - d))

    at_z = [lax.rem(my_z + d, z_size) for d in outward(z_size)]
    at_y = [lax.rem(my_y + d, y_size) * z_size for d in outward(y_size)]
    peers = [z + y for z in at_z for y in at_y][: n_sta - 1]
    tpl_peers = [lax.rem(my_t + o, n_tpl) for o in range(1, n_tpl)]

    barrier = pltpu.get_barrier_semaphore()

    for peer in peers:
        pl.semaphore_signal(barrier, inc=1, device_id={"sta": peer}, device_id_type=MESH)
    for peer in tpl_peers:
        pl.semaphore_signal(barrier, inc=1, device_id={"tpl": peer}, device_id_type=MESH)
    inputs = [
        pltpu.make_async_copy(src, dst, in_sem.at[n])
        for n, (src, dst) in enumerate(
            [
                (chan_hbm, chan_ref),
                (count_hbm, count_ref),
                (table_hbm, table_ref),
                (waves_hbm, waves_ref),
                (window_hbm, window_ref),
                (prior_hbm, prior_ref),
            ]
        )
    ]
    for copy in inputs:
        copy.start()
    for copy in inputs:
        copy.wait()

    square = (positions, positions)
    lane = iota(square, 1)
    sub = iota(square, 0)
    lane1 = iota((1, positions), 1)
    template = lane1 % group

    def to_rows(row):
        return jnp.broadcast_to(row, square).T

    chan = jnp.concatenate([chan_ref[j : j + 1, :] for j in range(slots)], axis=1)
    counts = jnp.concatenate([count_ref[...]] * slots, axis=1)
    station = (chan * 43691) >> 17
    station_rows = to_rows(station)
    looked = jnp.zeros(square, I32)
    for h in range(table_ref.shape[1] // LANES):
        entries = jnp.broadcast_to(table_ref[:, pl.ds(LANES * h, LANES)], square)
        looked = jnp.where(station_rows == lane + LANES * h, entries, looked)
    looked = jnp.sum(looked.T, axis=0, keepdims=True)
    block_stations = rows // 3
    owner = looked // block_stations
    local = 3 * (looked % block_stations) + chan - 3 * station
    cap = positions // n_sta
    before = (to_rows(owner) == owner) & (sub < lane)
    rank = jnp.sum(jnp.where(before, 1, 0), axis=0, keepdims=True)
    slot_at = owner * cap + rank
    place = sub == slot_at
    listed = jnp.where(me * slots + lane1 // group < counts, 1.0, 0.0)
    code_rows = to_rows(local * group + template)
    mrow[...] = jnp.sum(jnp.where(to_rows(slot_at) == lane, code_rows, 0), axis=0, keepdims=True)

    for t in range(0, group):
        wave = waves_ref[t].astype(F32)
        wave = jnp.concatenate([wave, jnp.zeros((slots, k_width - length), F32)], axis=1)
        for r in range(k_blocks):
            flat[r, pl.ds(t, slots, stride=group), :] = wave[:, LANES * r : LANES * (r + 1)]
    mover = jnp.where(place, jnp.broadcast_to(listed, (positions, positions)), 0.0).astype(BF16)
    moved = jnp.concatenate(
        [dot(mover, flat[r].astype(BF16), NN) for r in range(k_blocks)], axis=1
    )
    norms = jnp.sqrt(jnp.sum(moved * moved, axis=1, keepdims=True) + EPSILON)
    normed = moved / norms
    for s in range(n_sta):
        sbuf[s] = normed[cap * s : cap * (s + 1)].astype(BF16)

    e_width = pl.cdiv(length + LANES - 1, LANES) * LANES
    ahead = iota((e_width, LANES), 0) - iota((e_width, LANES), 1)
    band[...] = jnp.where((ahead >= 0) & (ahead < length), 1.0, 0.0).astype(BF16)

    pl.semaphore_wait(barrier, n_sta + n_tpl - 2)

    def remote(src, dst, send, recv, device):
        return pltpu.make_async_remote_copy(
            src_ref=src,
            dst_ref=dst,
            send_sem=send,
            recv_sem=recv,
            device_id=device,
            device_id_type=MESH,
        )

    def win_copy(slot, peer):
        return remote(window_ref, win.at[slot], win_send.at[peer], win_recv.at[slot], {"tpl": peer})

    def wave_copy(k, peer):
        return remote(
            sbuf.at[peer], rbuf.at[k], wave_send, wave_recv.at[k // BATCH], {"sta": peer}
        )

    def meta_copy(k, peer):
        return remote(
            mrow, mbuf.at[k], meta_send, meta_recv.at[k // BATCH], {"sta": peer}
        )

    def res_copy(k, peer):
        return remote(obuf.at[peer], rres.at[k], res_send, res_recv, {"sta": peer})

    def over_tpl(body):
        for peer in tpl_peers:
            body(peer)

    def over_sta(body):
        for k, peer in enumerate(peers):
            body(k, peer)

    batches = n_sta // BATCH

    def batch_of(g):
        return pl.ds(BATCH * g, BATCH - 1 if g == batches - 1 else BATCH)

    over_tpl(lambda peer: win_copy(my_t, peer).start())
    for k, peer in reversed(list(enumerate(peers))):
        meta_copy(k, peer).start()
    for k, peer in reversed(list(enumerate(peers))):
        wave_copy(k, peer).start()
    win[my_t] = window_ref[...]
    rbuf[n_sta - 1] = sbuf[me]
    mbuf[n_sta - 1] = mrow[...]

    quarter = iota((8, LANES), 1) // SUB

    def pick(parts):
        value = parts[0]
        for i in range(1, QUARTERS):
            value = jnp.where(quarter == i, parts[i], value)
        return value

    def shift_waves(s):
        wave = rbuf[s].astype(F32)
        return jnp.concatenate(
            [
                pltpu.roll(
                    jnp.broadcast_to(wave[i : i + 1], (SUB, k_width)), 0, 1, stride=1, stride_axis=0
                )
                for i in range(cap)
            ],
            axis=0,
        ).astype(BF16)

    def correlate(s, shifted):
        codes = [msm[s, 0, cap * me + i] for i in range(cap)]
        local_rows = [code >> (group.bit_length() - 1) for code in codes]
        data = jnp.concatenate([xall[c] for c in local_rows], axis=0)
        found = dot(data, shifted, NT)
        block = lambda i, b: found[SUB * i + cells * b : SUB * i + cells * (b + 1)]
        turned = []
        for d in range(QUARTERS):
            v = pick([block(i, (i + d) % QUARTERS) for i in range(cap)])
            turned.append(v if d == 0 else pltpu.roll(v, SUB * d, 1))
        out = []
        for i in range(cap):
            v = pick([turned[(b - i) % QUARTERS] for b in range(QUARTERS)])
            out.append(v * sc[local_rows[i]])
        traces = jnp.concatenate(out, axis=0)
        hi = traces.astype(BF16)
        lo = (traces - hi.astype(F32)).astype(BF16)
        here = pl.ds(cells * cap * s, cells * cap)
        ohl[here, pl.ds(0, LANES)] = hi
        ohl[here, pl.ds(LANES, LANES)] = lo

    def to_scalars(g):
        here = pl.ds(BATCH * g, BATCH)
        return pltpu.make_async_copy(mbuf.at[here], msm.at[here], sm_sem.at[g])

    def meta_here(g):
        here = batch_of(g)
        remote(mbuf.at[here], mbuf.at[here], meta_send, meta_recv.at[g], {"sta": me}).wait_recv()
        to_scalars(g).start()

    def waves_here(g):
        here = batch_of(g)
        remote(rbuf.at[here], rbuf.at[here], wave_send, wave_recv.at[g], {"sta": me}).wait_recv()

    first = batches - 1
    meta_here(first)
    lane_p = iota((PACK, LANES), 1)
    prior_tiles = prior_len // LANES
    prior_rest = prior_len % LANES

    def square_parts(x):
        square = x * x
        high = square.astype(BF16)
        return high, (square - high.astype(F32)).astype(BF16)

    def keep(g, b, m, value):
        xs[b, pl.ds(pitch * PACK * g + m, PACK, stride=pitch), :] = value

    old_width = prior_tiles * LANES
    for g in range(rows // PACK):
        here = pl.ds(PACK * g, PACK)
        old = prior_ref[here, :][:, :old_width].astype(F32)
        for b in range(QUARTERS):
            moved_x = shift_left(old, SUB * b)
            for m in range(prior_tiles if b == 0 else prior_tiles - 1):
                keep(g, b, m, moved_x[:, LANES * m : LANES * (m + 1)])
        squares[here, pl.ds(0, old_width)], squares[
            pl.ds(rows + PACK * g, PACK), pl.ds(0, old_width)
        ] = square_parts(old)

    over_tpl(lambda peer: win_copy(peer, peer).wait_recv())

    for g in range(rows // PACK):
        here = pl.ds(PACK * g, PACK)
        first_tile = prior_tiles - 1
        old = prior_ref[here, :][:, first_tile * LANES :].astype(F32)
        new = jnp.concatenate(
            [win[p, here, :].astype(F32) for p in range(n_tpl)] + [jnp.zeros((PACK, LANES), F32)],
            axis=1,
        )
        new = pltpu.roll(new, prior_rest, 1)
        tail = jnp.concatenate(
            [old[:, LANES:], jnp.zeros((PACK, LANES - prior_rest), F32)], axis=1
        )
        joint = jnp.where(lane_p < prior_rest, tail, new[:, :LANES])
        x = jnp.concatenate([old[:, :LANES], joint, new[:, LANES:]], axis=1)
        for b in range(QUARTERS):
            moved_x = shift_left(x, SUB * b)
            for m in range(prior_tiles if b == 0 else first_tile, x_blocks):
                at = m - first_tile
                keep(g, b, m, moved_x[:, LANES * at : LANES * (at + 1)])
        newer = pl.ds(old_width, (x_blocks - prior_tiles) * LANES)
        squares[here, newer], squares[pl.ds(rows + PACK * g, PACK), newer] = square_parts(
            x[:, LANES:]
        )

    energy = dot(
        jnp.concatenate([squares[:, pl.ds(LANES * a, e_width)] for a in range(cells)], axis=0),
        band[...],
        NN,
    )
    for a in range(cells):
        high_part = energy[2 * rows * a : 2 * rows * a + rows]
        low_part = energy[2 * rows * a + rows : 2 * rows * (a + 1)]
        sc[:, a, :] = 1.0 / jnp.sqrt(high_part + low_part + EPSILON)

    def build_row(c, _):
        for r in range(k_blocks):
            for b in range(0, QUARTERS, 2):
                pair = jnp.concatenate(
                    [xs[b + d, pl.ds(pitch * c + r, cells), :] for d in range(2)], axis=0
                )
                xall[c, pl.ds(cells * b, 2 * cells), pl.ds(LANES * r, LANES)] = pair.astype(BF16)
        return 0

    lax.fori_loop(0, rows, build_row, 0, unroll=4)

    for g in reversed(range(batches)):
        if g:
            meta_here(g - 1)
        waves_here(g)
        to_scalars(g).wait()
        for k in range(BATCH):
            correlate(BATCH * g + k, shift_waves(BATCH * g + k))

    codes = mbuf[...].reshape(n_sta, LANES)
    mine = pltpu.roll(codes, lax.rem(positions - cap * me, positions), 1)
    tmpl = mine & (group - 1)
    lane_s = iota((n_sta, LANES), 1)
    sub_s = iota((n_sta, LANES), 0)
    by_lane = jnp.zeros((n_sta, LANES), I32)
    for j in range(cap):
        by_lane = jnp.where(
            (lane_s // cells) % cap == j, jnp.broadcast_to(tmpl[:, j : j + 1], (n_sta, LANES)), by_lane
        )
    per_tile = LANES // (cap * cells)
    by_lane = by_lane.astype(F32)
    out_rows = group * cells
    row_t = (iota((out_rows, LANES), 0) // cells).astype(F32)
    same_a = iota((out_rows, LANES), 0) % cells == iota((out_rows, LANES), 1) % cells
    tiles = []
    for m in range(positions * cells // LANES):
        names = jnp.sum(
            jnp.where(sub_s == per_tile * m + lane_s // (cap * cells), by_lane, 0.0),
            axis=0,
            keepdims=True,
        )
        tiles.append(jnp.where((row_t == names) & same_a, 1.0, 0.0).astype(BF16))
    chooser = jnp.concatenate(tiles, axis=1)
    both = dot(chooser, ohl[...], NN)
    stacked = both[:, :LANES] + both[:, LANES:]
    for t in range(group):
        obuf[t] = stacked[cells * t : cells * (t + 1)]

    over_sta(lambda k, peer: res_copy(k, peer).start())
    rres[n_sta - 1] = obuf[me]
    others = pl.ds(0, n_sta - 1)
    over_tpl(lambda peer: win_copy(my_t, peer).wait_send())
    remote(mbuf.at[others], mbuf.at[others], meta_send, meta_recv.at[0], {"sta": me}).wait_send()
    remote(sbuf.at[others], sbuf.at[others], wave_send, wave_recv.at[0], {"sta": me}).wait_send()
    results = remote(obuf.at[others], rres.at[others], res_send, res_recv, {"sta": me})
    results.wait_send()
    results.wait_recv()
    total = jnp.sum(rres[...], axis=0)
    for a in range(cells):
        out_ref[0:1, pl.ds(LANES * a, LANES)] = total[a : a + 1]


def solution(mesh):
    n_sta, n_tpl = mesh.shape["sta"], mesh.shape["tpl"]

    def per_device(window, prior, waves, chan_list, chan_count, station_row):
        group, slots, length = waves.shape
        rows = window.shape[0]
        lags = window.shape[1] * n_tpl
        positions = group * slots
        cap = positions // n_sta
        cells = lags // LANES
        k_width = pl.cdiv(length + SUB - 1, LANES) * LANES
        cfg = (n_sta, n_tpl, group, slots, length, rows, lags, 8)
        vmem = pl.BlockSpec(memory_space=pltpu.VMEM)
        dma = pltpu.SemaphoreType.DMA
        return pl.pallas_call(
            functools.partial(kernel, cfg),
            out_shape=pltpu.VMEM((1, lags), F32),
            in_specs=[pl.BlockSpec(memory_space=pl.ANY)] * 6,
            out_specs=vmem,
            scratch_shapes=[
                pltpu.VMEM(window.shape, BF16),
                pltpu.VMEM(prior.shape, BF16),
                pltpu.VMEM(waves.shape, BF16),
                pltpu.VMEM((slots, group), I32),
                pltpu.VMEM((1, group), I32),
                pltpu.VMEM((1, station_row.shape[0]), I32),
                pltpu.VMEM((n_tpl, rows, window.shape[1]), BF16),
                pltpu.VMEM((k_width // LANES, positions, LANES), F32),
                pltpu.VMEM((n_sta, cap, k_width), BF16),
                pltpu.VMEM((n_sta, cap, k_width), BF16),
                pltpu.VMEM((pl.cdiv(length + LANES - 1, LANES) * LANES, LANES), BF16),
                pltpu.VMEM((2 * rows, pl.cdiv(length - 1 + lags, LANES) * LANES), BF16),
                pltpu.VMEM((1, positions), I32),
                pltpu.VMEM((n_sta, 1, positions), I32),
                pltpu.SMEM((n_sta, 1, positions), I32),
                pltpu.VMEM((QUARTERS, rows * pl.cdiv(length - 1 + lags, LANES), LANES), F32),
                pltpu.VMEM((rows, SUB, k_width), BF16),
                pltpu.VMEM((rows, cells, LANES), F32),
                pltpu.VMEM((positions * cells, 2 * LANES), BF16),
                pltpu.VMEM((group, cells, LANES), F32),
                pltpu.VMEM((n_sta, cells, LANES), F32),
                dma((n_tpl,)),
                dma((n_tpl,)),
                dma(()),
                dma((n_sta // BATCH,)),
                dma(()),
                dma((n_sta // BATCH,)),
                dma(()),
                dma(()),
                dma((n_sta // BATCH,)),
                dma((6,)),
            ],
            compiler_params=pltpu.CompilerParams(collective_id=0, has_side_effects=True),
        )(
            window,
            prior,
            waves,
            chan_list.T,
            chan_count.reshape(1, group),
            station_row.reshape(1, -1),
        )

    return jax.shard_map(
        per_device,
        mesh=mesh,
        in_specs=(
            P("sta", "tpl"),
            P("sta", None),
            P("tpl", "sta", None),
            P("tpl", "sta"),
            P("tpl"),
            P(),
        ),
        out_specs=P(("tpl", "sta"), None),
        check_vma=False,
    )
```
